256 devices in a mesh: seq: 256 (over y, x, z, core).
Axes of the slice: x: 4, y: 4, z: 8, core: 2. Of those that a mesh axis runs over, the one named last changes fastest.
Arguments:
- queries: bfloat16 [98304, 1024], P('seq'), may hold values from -125 to 125, as said below
- keys_values: bfloat16 [2, 98304, 1024], P(None, 'seq'), may hold values from -6 to 6, as said below
- rand_blocks: int32 [768, 3], P('seq'), may hold values from 0 to 47, as said below
- global_ids: int32 [2], replicated, may hold values from 0 to 767
- out_weight: bfloat16 [1024, 2048], replicated, may hold values from -0.1875 to 0.1875
Outputs:
- layer_out: bfloat16 [98304, 2048], P('seq')
The draws below stay inside these ranges and needn't reach their ends.
Inputs may be any that keep to these rules, and one draw needn't show every extreme that they name: queries stay within the range. `keys_values`: keys and values stay within the range. `rand_blocks`: entry e names the block held by the segment's device number e // 3. Among the 9 entries of the rows of one device (aligned blocks of 3 rows), no segment device is named more than 1 times, and some segment device is named exactly 1 times.
All inputs are finite; a program needn't handle non-finite values.
Results may differ from the reference program's by a relative error of at most 0.0057.
Values may be sent and summed in bfloat16 or wider, within the bound.
A program may use at most 192 MiB of HBM per device.

```python
import math
import jax
import jax.numpy as jnp
from jax import lax

D = 2048
HEADS = 8
HEAD_DIM = 128
BLOCK = 128
RAND = 3
GLOB = 2
SEG_DEV = 16
INNER = 1024
BLK_DEV = 3
SEG_BLK = 48
TOKENS = 98304
NBLK = 768


def shared_fields(key):
    keys_part = jnp.clip(jax.random.normal(jax.random.fold_in(key, 11), (TOKENS, INNER), jnp.float32), -6.0, 6.0)
    query_part = jnp.clip(jax.random.normal(jax.random.fold_in(key, 12), (TOKENS, INNER), jnp.float32), -6.0, 6.0)
    return (keys_part, query_part)


def draw_keys_values(key, part):
    keys_part, query_part = shared_fields(key)
    value_part = jnp.clip(jax.random.normal(jax.random.fold_in(key, 13), (TOKENS, INNER), jnp.float32), -6.0, 6.0)
    return jnp.stack([keys_part, value_part]).astype(jnp.bfloat16)


def draw_queries(key, part):
    keys_part, query_part = shared_fields(key)
    return query_part.astype(jnp.bfloat16)


def draw_rand_blocks(key, part):
    device_count = NBLK // BLK_DEV
    slot_count = BLK_DEV * RAND
    order_keys = jax.random.split(jax.random.fold_in(key, 21), device_count)

    def device_owners(one_key):
        ordering = jax.random.permutation(one_key, SEG_DEV).astype(jnp.int32)
        slot_index = jnp.arange(slot_count, dtype=jnp.int32)
        return jnp.take(ordering, slot_index % SEG_DEV)
    owners = jax.vmap(device_owners)(order_keys)
    local_ids = jax.random.randint(jax.random.fold_in(key, 22), (device_count, slot_count), 0, BLK_DEV).astype(jnp.int32)
    return (owners * BLK_DEV + local_ids).reshape(NBLK, RAND).astype(jnp.int32)


def centred(key, shape, scale, limit, held_as=jnp.bfloat16):
    entries = scale * jax.random.normal(key, shape, jnp.float32)
    return jnp.clip(entries, min=-limit, max=limit).astype(held_as)


def setup_inputs(seed: int = 0) -> dict:
    seeds = jax.random.split(jax.random.key(seed), 6)
    queries = draw_queries(jax.random.fold_in(seeds[5], 71), 0)
    keys_values = draw_keys_values(jax.random.fold_in(seeds[5], 71), 0)
    rand_blocks = draw_rand_blocks(jax.random.fold_in(seeds[5], 71), 0)
    global_ids = jax.random.randint(seeds[3], (GLOB,), 0, NBLK).astype(jnp.int32)
    out_weight = centred(seeds[4], (INNER, D), INNER ** -0.5, 0.1875)
    return dict(queries=queries, keys_values=keys_values, rand_blocks=rand_blocks, global_ids=global_ids, out_weight=out_weight)


def reference(queries, keys_values, rand_blocks, global_ids, out_weight):
    inner_width = queries.shape[1]
    scale_factor = 1.0 / math.sqrt(HEAD_DIM)
    query_blocks = queries.reshape(NBLK, BLOCK, HEADS, HEAD_DIM)
    pair_blocks = keys_values.reshape(2, NBLK, BLOCK, inner_width)

    def attend_block(block_index):
        seg_start = block_index // SEG_BLK * SEG_BLK
        window_ids = jnp.stack([(block_index - 1) % NBLK, block_index, (block_index + 1) % NBLK]).astype(jnp.int32)
        key_blocks = jnp.concatenate([window_ids, global_ids.astype(jnp.int32), (seg_start + rand_blocks[block_index]).astype(jnp.int32)])
        chosen = pair_blocks[:, key_blocks].reshape(2, 8 * BLOCK, HEADS, HEAD_DIM)
        query_now = query_blocks[block_index]
        scores = jnp.einsum('qhd,khd->hqk', query_now.astype(jnp.float32), chosen[0].astype(jnp.float32)) * scale_factor
        probs = jax.nn.softmax(scores, axis=-1).astype(jnp.bfloat16)
        attended = jnp.einsum('hqk,khd->qhd', probs.astype(jnp.float32), chosen[1].astype(jnp.float32))
        return attended.astype(jnp.bfloat16).reshape(BLOCK, inner_width)
    attended_all = lax.map(attend_block, jnp.arange(NBLK, dtype=jnp.int32))
    attended_all = attended_all.reshape(NBLK * BLOCK, inner_width)
    return jnp.dot(attended_all, out_weight, preferred_element_type=jnp.float32).astype(jnp.bfloat16)
```

```python
import functools
import math

import jax
import jax.numpy as jnp
from jax import lax
from jax.experimental import pallas as pl
from jax.experimental.pallas import tpu as pltpu
from jax.sharding import PartitionSpec as P

HEADS = 8
HEAD_DIM = 128
BLOCK = 128
BLK_DEV = 3
SEG_DEV = 16
SEG_BLK = SEG_DEV * BLK_DEV
RING = 8
PLANE = 32
CHUNKS = 2 * BLK_DEV
EDGE = SEG_BLK
GLOBAL = SEG_BLK + 1
SLOTS = SEG_BLK + 3
SLICE = 16
MESH = pl.DeviceIdType.MESH


def remote(src, dst, send, recv, device):
    return pltpu.make_async_remote_copy(
        src_ref=src, dst_ref=dst, send_sem=send, recv_sem=recv, device_id=(device,), device_id_type=MESH
    )


def gather_kernel(
    owner_ref, kv_ref, cand_ref, out_ref, own, recv1, recv2, sel1, sel2,
    local_sem, ring_send, ring_recv, pair_send, pair_recv, edge_send, edge_recv,
    s1, r1, s2, r2, s3, r3,
):
    me = lax.axis_index("seq")
    core = me % 2
    z = me // 2 % RING
    seg = me // SEG_DEV
    plane = seg * 2 + core
    other = me + 1 - 2 * core
    home = me % SEG_DEV

    def at_z(zz):
        return seg * SEG_DEV + zz * 2 + core

    def at_plane(p):
        return p // 2 * SEG_DEV + z * 2 + p % 2

    barrier = pltpu.get_barrier_semaphore()

    @pl.loop(1, PLANE)
    def _(i):
        pl.semaphore_signal(barrier, inc=1, device_id=(at_plane((plane + i) % PLANE),), device_id_type=MESH)

    @pl.loop(1, RING)
    def _(i):
        pl.semaphore_signal(barrier, inc=1, device_id=(at_z((z + i) % RING),), device_id_type=MESH)

    pl.semaphore_wait(barrier, PLANE - 1 + RING - 1)

    def kv_chunk(q):
        return kv_ref.at[q // BLK_DEV, pl.ds(pl.multiple_of(q % BLK_DEV * BLOCK, BLOCK), BLOCK)]

    def slot(device, q):
        return out_ref.at[device * BLK_DEV + q % BLK_DEV, q // BLK_DEV]

    steps = (1, RING - 1)

    def ring(way, hop, q):
        held = (z + (hop - 1) * (RING - steps[way])) % RING * 2 + core
        src = kv_chunk(q) if hop == 1 else slot(held, q)
        return remote(
            src, slot(held, q), ring_send.at[way, hop - 1, q], ring_recv.at[way, hop - 1, q], at_z((z + steps[way]) % RING)
        )

    def came(way, hop, q):
        source = (z + hop * (RING - steps[way])) % RING * 2 + core
        here = slot(source, q)
        return remote(here, here, ring_send.at[way, hop - 1, q], ring_recv.at[way, hop - 1, q], other), source

    def pair(index, src, block, q):
        return remote(src, slot(block, q), pair_send.at[index, q], pair_recv.at[index, q], other)

    for q in range(CHUNKS):
        for way in range(2):
            ring(way, 1, q).start()
    bring = pltpu.make_async_copy(kv_ref, own, local_sem.at[0])
    bring.start()

    @pl.loop(1, PLANE)
    def _(i):
        to = (plane + i) % PLANE
        remote(cand_ref.at[to], recv1.at[plane], s1.at[to], r1.at[plane], at_plane(to)).start()

    mine = pltpu.make_async_copy(cand_ref.at[plane], recv1.at[plane], local_sem.at[1])
    mine.start()
    for q in range(CHUNKS):
        pair(0, kv_chunk(q), home, q).start()
    bring.wait()

    def keep(q):
        return pltpu.make_async_copy(
            own.at[q // BLK_DEV, pl.ds(q % BLK_DEV * BLOCK, BLOCK)], slot(home, q), local_sem.at[2 + q]
        )

    for q in range(CHUNKS):
        keep(q).start()

    def arrive(way, hop, q):
        got, source = came(way, hop, q)
        got.wait_recv()
        last = RING // 2 - 1
        if hop < last or (hop == last and (q < BLK_DEV) == (way == 0)):
            ring(way, hop + 1, q).start()
        index = hop if way == 0 or hop > last else hop + RING // 2
        pair(index, slot(source, q), source, q).start()

    def hop_of(hop):
        for q in range(CHUNKS):
            for way in range(2):
                if hop < RING // 2 or (q < BLK_DEV) == (way == 0):
                    arrive(way, hop, q)

    hop_of(1)

    def edge(block, kv, device):
        return remote(out_ref.at[block, kv], out_ref.at[EDGE, kv], edge_send.at[kv], edge_recv.at[kv], device)

    count = 16 * SEG_DEV
    up = (z == 0) & (core == 1)
    down = (z == RING - 1) & (core == 0)

    @pl.when(up)
    def _():
        for kv in range(2):
            edge(SEG_BLK - 1, kv, (me + SEG_DEV - 1) % count).start()

    @pl.when(down)
    def _():
        for kv in range(2):
            edge(0, kv, (me + count - SEG_DEV + 1) % count).start()

    mine.wait()

    @pl.loop(1, PLANE)
    def _(i):
        src = (plane + i) % PLANE
        remote(cand_ref.at[src], recv1.at[src], s1.at[src], r1.at[src], other).wait_recv()

    sel1[...] = recv1[owner_ref[0]]
    hop_of(2)

    @pl.loop(1, RING)
    def _(i):
        to = (z + i) % RING
        remote(sel1, recv2.at[z], s2.at[to], r2.at[z], at_z(to)).start()

    recv2[z] = sel1[...]

    @pl.loop(1, RING)
    def _(i):
        src = (z + i) % RING
        remote(sel1, recv2.at[src], s2.at[src], r2.at[src], other).wait_recv()

    sel2[...] = recv2[owner_ref[1]]

    def global_slot(p):
        return out_ref.at[
            GLOBAL + p // 16, p // 8 % 2, pl.ds(pl.multiple_of(p % 8 * SLICE, SLICE), SLICE)
        ]

    hop_of(3)

    @pl.loop(1, PLANE)
    def _(i):
        to = (plane + i) % PLANE
        remote(sel2, global_slot(plane), s3.at[to], r3.at[plane], at_plane(to)).start()

    own_slice = pltpu.make_async_copy(sel2, global_slot(plane), local_sem.at[1])
    own_slice.start()
    hop_of(4)

    own_slice.wait()
    for q in range(CHUNKS):
        keep(q).wait()

    @pl.loop(1, PLANE)
    def _(i):
        at = (plane + i) % PLANE
        remote(sel2, global_slot(at), s3.at[at], r3.at[at], other).wait_recv()
        remote(sel2, global_slot(plane), s3.at[at], r3.at[at], other).wait_send()
        remote(cand_ref.at[at], recv1.at[at], s1.at[at], r1.at[at], other).wait_send()

    @pl.loop(1, RING)
    def _(i):
        at = (z + i) % RING
        remote(sel1, recv2.at[at], s2.at[at], r2.at[at], other).wait_send()

    @pl.when((z == 0) & (core == 0) | (z == RING - 1) & (core == 1))
    def _():
        for kv in range(2):
            edge(0, kv, other).wait_recv()

    @pl.when(up | down)
    def _():
        for kv in range(2):
            edge(0, kv, other).wait_send()

    for q in range(CHUNKS):
        for way in range(2):
            for hop in range(1, RING // 2 + 1):
                if hop < RING // 2 or (q < BLK_DEV) == (way == 0):
                    ring(way, hop, q).wait_send()
        for index in range(RING):
            twin = home + 1 - 2 * core
            turn = index if index <= RING // 2 else RING - (index - RING // 2)
            block = (z + RING - turn) % RING * 2 + 1 - core if index else twin
            there = slot(block, q)
            copy = remote(there, there, pair_send.at[index, q], pair_recv.at[index, q], other)
            copy.wait_recv()
            copy.wait_send()


def gather(owner, kv, cand):
    dma = pltpu.SemaphoreType.DMA
    bf16 = jnp.bfloat16
    width = kv.shape[2]
    return pl.pallas_call(
        gather_kernel,
        out_shape=jax.ShapeDtypeStruct((SLOTS, 2, BLOCK, width), bf16),
        in_specs=[
            pl.BlockSpec(memory_space=pltpu.SMEM),
            pl.BlockSpec(memory_space=pl.ANY),
            pl.BlockSpec(memory_space=pl.ANY),
        ],
        out_specs=pl.BlockSpec(memory_space=pl.ANY),
        scratch_shapes=[
            pltpu.VMEM(kv.shape, bf16),
            pltpu.VMEM((PLANE, SLICE, width), bf16),
            pltpu.VMEM((RING, SLICE, width), bf16),
            pltpu.VMEM((SLICE, width), bf16),
            pltpu.VMEM((SLICE, width), bf16),
            dma((2 + CHUNKS,)),
            dma((2, RING // 2, CHUNKS)), dma((2, RING // 2, CHUNKS)),
            dma((RING, CHUNKS)), dma((RING, CHUNKS)),
            dma((2,)), dma((2,)),
            dma((PLANE,)), dma((PLANE,)),
            dma((RING,)), dma((RING,)),
            dma((PLANE,)), dma((PLANE,)),
        ],
        compiler_params=pltpu.CompilerParams(collective_id=0, has_side_effects=True),
        name="gather_blocks",
    )(owner, kv, cand)


def attend_kernel(table_ref, q_ref, *refs):
    kv_refs, (w_ref, o_ref, att) = refs[:8], refs[8:]
    scale = math.log2(math.e) / math.sqrt(HEAD_DIM)
    for head in range(HEADS):
        cols = pl.ds(head * HEAD_DIM, HEAD_DIM)
        keys = jnp.concatenate([ref[0, 0, :, cols] for ref in kv_refs], axis=0)
        values = jnp.concatenate([ref[0, 1, :, cols] for ref in kv_refs], axis=0)
        scores = lax.dot_general(
            q_ref[:, cols], keys, (((1,), (1,)), ((), ())), preferred_element_type=jnp.float32
        ) * scale
        top = jnp.max(scores, axis=1, keepdims=True)
        probs = jnp.exp2(scores - top)
        total = jnp.sum(probs, axis=1, keepdims=True)
        out = jnp.dot(probs.astype(jnp.bfloat16), values, preferred_element_type=jnp.float32)
        att[:, cols] = (out / total).astype(jnp.bfloat16)
    o_ref[...] = jnp.dot(att[...], w_ref[...], preferred_element_type=jnp.float32).astype(o_ref.dtype)


def attend(table, queries, blocks, weight):
    rows, width = queries.shape
    depth = weight.shape[1]

    def kv_spec(i):
        return pl.BlockSpec((1, 2, BLOCK, width), lambda b, t: (t[b * 8 + i], 0, 0, 0))

    return pl.pallas_call(
        attend_kernel,
        out_shape=jax.ShapeDtypeStruct((rows, depth), jnp.bfloat16),
        grid_spec=pltpu.PrefetchScalarGridSpec(
            num_scalar_prefetch=1,
            grid=(rows // BLOCK,),
            in_specs=[pl.BlockSpec((BLOCK, width), lambda b, t: (b, 0))]
            + [kv_spec(i) for i in range(8)]
            + [pl.BlockSpec((width, depth), lambda b, t: (0, 0), pipeline_mode=pl.Buffered(1))],
            out_specs=pl.BlockSpec((BLOCK, depth), lambda b, t: (b, 0)),
            scratch_shapes=[pltpu.VMEM((BLOCK, width), jnp.bfloat16)],
        ),
        compiler_params=pltpu.CompilerParams(vmem_limit_bytes=60 << 20),
        name="attend_blocks",
    )(table, queries, *([blocks] * 8), weight)


def local(queries, keys_values, rand_blocks, global_ids, out_weight):
    device = lax.axis_index("seq")
    home = device % SEG_DEV
    width = queries.shape[1]
    plane = device // SEG_DEV * 2 + device % 2
    owner = global_ids // BLK_DEV
    chosen = jnp.where(plane < PLANE // 2, owner[0], owner[1])
    owner_at = jnp.stack([chosen // SEG_DEV * 2 + chosen % 2, chosen // 2 % RING])
    cand = jnp.stack(
        [
            lax.dynamic_slice_in_dim(keys_values, global_ids[g] % BLK_DEV * BLOCK, BLOCK, 1)
            for g in range(2)
        ]
    ).reshape(PLANE, SLICE, width)
    blocks = gather(owner_at, keys_values, cand)
    first = home * BLK_DEV
    near = first + jnp.arange(BLK_DEV, dtype=jnp.int32)[:, None] + jnp.arange(-1, 2, dtype=jnp.int32)[None]
    near = jnp.where((near < 0) | (near >= SEG_BLK), EDGE, near)
    wide = jnp.broadcast_to(jnp.array([GLOBAL, GLOBAL + 1], jnp.int32), (BLK_DEV, 2))
    table = jnp.concatenate([near, wide, rand_blocks], axis=1).reshape(-1)
    return attend(table, queries, blocks, out_weight)


def solution(mesh):
    placed = (P("seq", None), P(None, "seq", None), P("seq", None), P(), P())
    return jax.shard_map(
        local, mesh=mesh, in_specs=placed, out_specs=P("seq", None), check_vma=False
    )
```

```python
import math

import jax
import jax.numpy as jnp
from jax import lax
from jax.experimental import pallas as pl
from jax.experimental.pallas import tpu as pltpu
from jax.sharding import PartitionSpec as P

HEADS = 8
HEAD_DIM = 128
BLOCK = 128
BLK_DEV = 3
RAND = 3
GLOB = 2
SEG_DEV = 16
SEGS = 16
RING = 8
PLANE = 32
CHUNKS = 2 * BLK_DEV
ENTRIES = BLK_DEV * RAND
EDGE = 10 * BLK_DEV
SLICE = 16
ROOT = 13 * SEG_DEV
SCALE = math.log2(math.e) / math.sqrt(HEAD_DIM)
MESH = pl.DeviceIdType.MESH
OWN, L1, L2, S1, S2, L3 = range(6)


def remote(src, dst, send, recv, device):
    return pltpu.make_async_remote_copy(
        src_ref=src, dst_ref=dst, send_sem=send, recv_sem=recv, device_id=(device,), device_id_type=MESH
    )


def kernel(
    rand_ref, ids_ref, q_hbm, kv_hbm, w_hbm, out_hbm,
    near, l3k, l3v, far, last, stage3, stage4, own, cand, recv1, recv2, sel1, sel2, glob,
    q_ref, w_ref, o_ent, e_ent, o_win, e_win, att, out_ref,
    tab_ls, tab_lo, tab_ss, tab_so, slots, ranks,
    load_sem, long_s, long_r, short_s, short_r, sel_s, sel_r, pair_s, pair_r, tab_s, tab_r, edge_s, edge_r,
    s1, r1, s2, r2, s3, r3, s4, r4, all_in,
):
    me = lax.axis_index("seq")
    core = me % 2
    z = me // 2 % RING
    seg = me // SEG_DEV
    home = me % SEG_DEV
    plane = seg * 2 + core
    other = me + 1 - 2 * core
    go_long = 1 + (RING - 2) * core
    go_short = RING - go_long

    def hop(steps):
        return (z + steps) % RING

    def at(zz, cc):
        return seg * SEG_DEV + zz * 2 + cc

    def at_plane(p):
        return p // 2 * SEG_DEV + z * 2 + p % 2

    loads = [pltpu.make_async_copy(kv_hbm.at[:, j], near.at[j], load_sem.at[j]) for j in range(BLK_DEV)]
    loads += [pltpu.make_async_copy(kv_hbm.at[:, j], own.at[j], load_sem.at[BLK_DEV + j]) for j in range(BLK_DEV)]
    load_q = pltpu.make_async_copy(q_hbm, q_ref, load_sem.at[6])
    load_w = pltpu.make_async_copy(w_hbm, w_ref, load_sem.at[7])
    for copy in loads + [load_q, load_w]:
        copy.start()

    barrier = pltpu.get_barrier_semaphore()

    @pl.loop(1, SEG_DEV)
    def _(i):
        pl.semaphore_signal(
            barrier, inc=1, device_id=(seg * SEG_DEV + (home + i) % SEG_DEV,), device_id_type=MESH
        )

    @pl.when(me != ROOT)
    def _():
        pl.semaphore_wait(barrier, SEG_DEV - 1)

    @pl.when(me == ROOT)
    def _():
        pl.semaphore_wait(barrier, SEG_DEV - 1 + SEGS - 1)

    def mine(shard, q):
        kv, j = q // BLK_DEV, q % BLK_DEV
        if shard == L3:
            return (l3v if kv else l3k).at[j]
        return near.at[shard * BLK_DEV + j, kv]

    def theirs(shard, q):
        kv, j = q // BLK_DEV, q % BLK_DEV
        if shard == L3:
            return far.at[j, kv]
        return near.at[(5 + shard) * BLK_DEV + j, kv]

    longs, shorts = (OWN, L1, L2, L3), (OWN, S1, S2)

    def long(h, q):
        return remote(
            mine(longs[h - 1], q), mine(longs[h], q), long_s.at[h - 1, q], long_r.at[h - 1, q], at(hop(go_long), core)
        )

    def short(h, q):
        return remote(
            mine(shorts[h - 1], q), mine(shorts[h], q), short_s.at[h - 1, q], short_r.at[h - 1, q],
            at(hop(go_short), core),
        )

    def pair(shard, q):
        return remote(mine(shard, q), theirs(shard, q), pair_s.at[shard, q], pair_r.at[shard, q], other)

    for copy in loads[:BLK_DEV]:
        copy.wait()
    for q in range(CHUNKS):
        long(1, q).start()
        short(1, q).start()
    tables = [
        remote(rand_ref, tab_ss, tab_s.at[0], tab_r.at[0], at(hop(go_long), core)),
        remote(rand_ref, tab_ls, tab_s.at[1], tab_r.at[1], at(hop(go_short), core)),
        remote(rand_ref, tab_lo, tab_s.at[2], tab_r.at[2], at(hop(go_long), 1 - core)),
        remote(rand_ref, tab_so, tab_s.at[3], tab_r.at[3], at(hop(go_short), 1 - core)),
    ]
    for copy in tables:
        copy.start()
    for q in range(CHUNKS):
        pair(OWN, q).start()

    head = home == 0

    @pl.when(head & (me != ROOT))
    def _():
        pl.semaphore_signal(barrier, inc=1, device_id=(ROOT,), device_id_type=MESH)

    @pl.when(me == ROOT)
    def _():
        @pl.loop(1, SEGS)
        def _(i):
            pl.semaphore_signal(
                all_in, inc=1, device_id=((seg + i) % SEGS * SEG_DEV,), device_id_type=MESH
            )

    for copy in loads[BLK_DEV:]:
        copy.wait()
    for g in range(GLOB):
        block = ids_ref[g] % BLK_DEV
        for kv in range(2):
            cand[pl.ds((g * 2 + kv) * 8, 8)] = own[block, kv].reshape(8, SLICE, HEADS * HEAD_DIM)

    def code_of(value):
        device = value // BLK_DEV
        delta = (device // 2 + RING - z) % RING
        behind = (delta * core + (RING - delta) * (1 - core)) % RING
        same = jnp.where(device % 2 == core, 1, 0)
        return same, jnp.where(same == 1, behind, (RING - behind) % RING)

    values = [rand_ref[e // RAND, e % RAND] for e in range(ENTRIES)]
    keys = []
    for value in values:
        same, u = code_of(value)
        keys.append(jnp.minimum(u, RING - u) * 32 + u * 2 + same)
    for e in range(ENTRIES):
        ranks[e] = sum(jnp.where(keys[f] < keys[e], 1, 0) for f in range(ENTRIES) if f != e)
    held = [ranks[e] for e in range(ENTRIES)]
    for i in range(ENTRIES):
        slots[i] = sum(jnp.where(held[e] == i, values[e] * 4 + e // RAND, 0) for e in range(ENTRIES))

    @pl.when(head)
    def _():
        @pl.when(me != ROOT)
        def _():
            pl.semaphore_wait(all_in, 1)

        @pl.loop(1, SEG_DEV)
        def _(i):
            pl.semaphore_signal(all_in, inc=1, device_id=(seg * SEG_DEV + i,), device_id_type=MESH)

    @pl.when(home != 0)
    def _():
        pl.semaphore_wait(all_in, 1)

    @pl.loop(1, PLANE)
    def _(i):
        to = (plane + i) % PLANE
        remote(cand.at[to], recv1.at[plane], s1.at[to], r1.at[plane], at_plane(to)).start()

    recv1[plane] = cand[plane]

    which = plane // 16
    owner = ids_ref[0] * (1 - which) + ids_ref[1] * which
    owner = owner // BLK_DEV

    def cols_of(zz):
        return pl.ds(pl.multiple_of(zz * 128, 128), 128)

    def choose_in_plane():
        @pl.loop(1, PLANE)
        def _(i):
            src = (plane + i) % PLANE
            remote(cand.at[src], recv1.at[src], s1.at[src], r1.at[src], other).wait_recv()

        sel1[...] = recv1[owner // SEG_DEV * 2 + owner % 2]

    def scatter_z():
        @pl.loop(1, RING)
        def _(i):
            to = (z + i) % RING
            remote(sel1.at[:, cols_of(to)], recv2.at[z], s2.at[to], r2.at[z], at(to, core)).start()

        recv2[z] = sel1[:, cols_of(z)]

    def choose_in_ring():
        @pl.loop(1, RING)
        def _(i):
            src = (z + i) % RING
            remote(recv2.at[src], recv2.at[src], s2.at[src], r2.at[src], other).wait_recv()

        sel2[:, cols_of(z)] = recv2[owner // 2 % RING]

    def gather_z():
        piece = sel2.at[:, cols_of(z)]

        @pl.loop(1, RING)
        def _(i):
            to = (z + i) % RING
            remote(piece, piece, s3.at[to], r3.at[z], at(to, core)).start()

    def global_slot(p):
        return glob.at[p // 16, p // 8 % 2, pl.ds(pl.multiple_of(p % 8 * SLICE, SLICE), SLICE)]

    def spread_in_plane():
        @pl.loop(1, RING)
        def _(i):
            src = (z + i) % RING
            piece = sel2.at[:, cols_of(src)]
            remote(piece, piece, s3.at[src], r3.at[src], other).wait_recv()

        @pl.loop(1, PLANE)
        def _(i):
            to = (plane + i) % PLANE
            remote(sel2, global_slot(plane), s4.at[to], r4.at[plane], at_plane(to)).start()

        glob[plane // 16, plane // 8 % 2, pl.ds(pl.multiple_of(plane % 8 * SLICE, SLICE), SLICE)] = sel2[...]

    def global_here():
        @pl.loop(1, PLANE)
        def _(i):
            src = (plane + i) % PLANE
            remote(sel2, global_slot(src), s4.at[src], r4.at[src], other).wait_recv()

    def arrive_long(h, q):
        long(h, q).wait_recv()
        if h < 3:
            long(h + 1, q).start()
        pair(longs[h], q).start()

    def arrive_short(h, q):
        short(h, q).wait_recv()
        if h < 2:
            short(h + 1, q).start()
        pair(shorts[h], q).start()

    def wanted(table, source):
        got = 0
        for e in range(ENTRIES):
            value = table[e // RAND, e % RAND]
            got += jnp.where(value // BLK_DEV == source, value % BLK_DEV, 0)
        return got

    def send_sel(third, twin, kv):
        way = go_short if third == 0 else go_long
        stage = (stage3, stage4)[third]
        land = far.at[BLK_DEV + twin, kv] if third == 0 else last.at[twin, kv]
        to = at(hop(way), core if twin == 0 else 1 - core)
        return remote(stage.at[twin, kv], land, sel_s.at[third, twin, kv], sel_r.at[third, twin, kv], to)

    def columns(head_index):
        return pl.ds(head_index * HEAD_DIM, HEAD_DIM)

    def attend(query, key, value):
        scores = lax.dot_general(query, key, (((1,), (1,)), ((), ())), preferred_element_type=jnp.float32) * SCALE
        top = jnp.max(scores, axis=1, keepdims=True)
        probs = jnp.exp2(scores - top)
        total = jnp.sum(probs, axis=1, keepdims=True)
        out = jnp.dot(probs.astype(jnp.bfloat16), value, preferred_element_type=jnp.float32)
        return out / total, jnp.broadcast_to(top + jnp.log2(total), out.shape)

    def entry(i, group):
        packed = slots[i]
        row, value = packed % 4, packed // 4
        same, u = code_of(value)
        j = value % BLK_DEV
        place = jnp.where(u <= 2, u, jnp.where(u == 7, S1, S2))
        is_near = (u <= 2) | (u >= 6)
        near_at = jnp.where(is_near, ((1 - same) * 5 + place) * BLK_DEV + j, 0)
        is_l3 = (u == 3) & (same == 1)
        is_far = ((u == 3) & (same == 0)) | (u == 5)
        far_at = jnp.where(u == 5, BLK_DEV + 1 - same, j)
        for head_index in range(HEADS):
            cols = columns(head_index)

            def fetch(kv):
                got = near[near_at, kv, :, cols]
                if group >= 1:
                    got = jnp.where(is_l3, (l3v if kv else l3k)[j, :, cols], got)
                    got = jnp.where(is_far, far[far_at, kv, :, cols], got)
                if group >= 2:
                    got = jnp.where(u == 4, last[1 - same, kv, :, cols], got)
                return got

            out, weight = attend(q_ref[row, :, cols], fetch(0), fetch(1))
            o_ent[i, :, cols] = out
            e_ent[i, :, cols] = weight

    def window(b):
        edge_low = (z == 0) & (core == 0)
        edge_high = (z == RING - 1) & (core == 1)
        before = jnp.where(core == 0, (5 + S1) * BLK_DEV + 2, 5 * BLK_DEV + 2)
        before = jnp.where(edge_low, EDGE, before)
        after = jnp.where(core == 0, 5 * BLK_DEV, (5 + S1) * BLK_DEV)
        after = jnp.where(edge_high, EDGE, after)
        places = [before, 0, 1, 2, after][b : b + 3]
        for head_index in range(HEADS):
            cols = columns(head_index)

            def fetch(kv):
                return jnp.concatenate(
                    [near[p, kv, :, cols] for p in places] + [glob[g, kv, :, cols] for g in range(GLOB)], axis=0
                )

            out, weight = attend(q_ref[b, :, cols], fetch(0), fetch(1))
            o_win[b, :, cols] = out
            e_win[b, :, cols] = weight

    for q in range(CHUNKS):
        arrive_long(1, q)
        arrive_short(1, q)
        if q == 3:
            choose_in_plane()
        if q == 4:
            scatter_z()

    count = SEGS * SEG_DEV
    up = (z == 0) & (core == 1)
    down = (z == RING - 1) & (core == 0)

    def edge(kv, device):
        return remote(
            near.at[S1 * BLK_DEV + 2 * core, kv], near.at[EDGE, kv], edge_s.at[kv], edge_r.at[kv], device
        )

    @pl.when(up)
    def _():
        for kv in range(2):
            edge(kv, (me + SEG_DEV - 1) % count).start()

    @pl.when(down)
    def _():
        for kv in range(2):
            edge(kv, (me + count - SEG_DEV + 1) % count).start()

    for q in range(CHUNKS):
        arrive_long(2, q)
        arrive_short(2, q)
        if q == 2:
            choose_in_ring()
        if q == 3:
            gather_z()
    for q in range(CHUNKS):
        for shard in (OWN, L1, S1, L2, S2):
            pair(shard, q).wait_recv()

    @pl.when((z == 0) & (core == 0) | (z == RING - 1) & (core == 1))
    def _():
        for kv in range(2):
            edge(kv, other).wait_recv()

    for copy, table in zip(tables, (tab_ss, tab_ls, tab_lo, tab_so)):
        copy.wait_recv()
    source = hop(2 * go_long) * 2 + core
    for twin, table in enumerate((tab_ss, tab_so)):
        block = S2 * BLK_DEV + wanted(table, source)
        for kv in range(2):
            stage3[twin, kv] = near[block, kv]
    spread_in_plane()
    load_q.wait()
    for kv in range(2):
        for twin in range(2):
            send_sel(0, twin, kv).start()

    @pl.loop(0, 3)
    def _(i):
        entry(i, 0)

    source = hop(3 * go_short) * 2 + core
    picks = [wanted(table, source) for table in (tab_ls, tab_lo)]
    for q in range(BLK_DEV):
        arrive_long(3, q)
    for twin in range(2):
        stage4[twin, 0] = l3k[picks[twin]]
    global_here()
    window(0)
    for twin in range(2):
        send_sel(1, twin, 0).start()
    window(1)
    window(2)
    for q in range(BLK_DEV, CHUNKS):
        arrive_long(3, q)
    for twin in range(2):
        stage4[twin, 1] = l3v[picks[twin]]
    for q in range(CHUNKS):
        pair(L3, q).wait_recv()
    for twin in range(2):
        send_sel(1, twin, 1).start()
    for kv in range(2):
        for twin in range(2):
            send_sel(0, twin, kv).wait_recv()

    @pl.loop(3, 7)
    def _(i):
        entry(i, 1)

    for q in range(CHUNKS):
        for h in range(1, 4):
            long(h, q).wait_send()
        for h in range(1, 3):
            short(h, q).wait_send()
        for shard in range(6):
            pair(shard, q).wait_send()
    for copy in tables:
        copy.wait_send()

    @pl.when(up | down)
    def _():
        for kv in range(2):
            edge(kv, other).wait_send()

    @pl.loop(1, PLANE)
    def _(i):
        to = (plane + i) % PLANE
        remote(cand.at[to], recv1.at[to], s1.at[to], r1.at[to], other).wait_send()
        remote(sel2, global_slot(plane), s4.at[to], r4.at[to], other).wait_send()

    @pl.loop(1, RING)
    def _(i):
        to = (z + i) % RING
        piece = sel1.at[:, cols_of(to)]
        remote(piece, piece, s2.at[to], r2.at[to], other).wait_send()
        piece = sel2.at[:, cols_of(z)]
        remote(piece, piece, s3.at[to], r3.at[to], other).wait_send()

    load_w.wait()

    for kv in range(2):
        for twin in range(2):
            send_sel(1, twin, kv).wait_recv()

    @pl.loop(7, ENTRIES)
    def _(i):
        entry(i, 2)

    stores = []
    for b in range(BLK_DEV):
        rows = [ranks[b * RAND + r] for r in range(RAND)]
        for head_index in range(HEADS):
            cols = columns(head_index)
            outs = [o_win[b, :, cols]] + [o_ent[r, :, cols] for r in rows]
            logs = [e_win[b, :, cols]] + [e_ent[r, :, cols] for r in rows]
            top = jnp.maximum(jnp.maximum(logs[0], logs[1]), jnp.maximum(logs[2], logs[3]))
            weights = [jnp.exp2(log - top) for log in logs]
            out = sum(w * o for w, o in zip(weights, outs)) / sum(weights)
            att[b, :, cols] = out.astype(jnp.bfloat16)
        out_ref[b] = jnp.dot(att[b], w_ref[...], preferred_element_type=jnp.float32).astype(jnp.bfloat16)
        store = pltpu.make_async_copy(out_ref.at[b], out_hbm.at[b], load_sem.at[b])
        store.start()
        stores.append(store)
    for kv in range(2):
        for twin in range(2):
            send_sel(0, twin, kv).wait_send()
            send_sel(1, twin, kv).wait_send()
    for store in stores:
        store.wait()


def local(queries, keys_values, rand_blocks, global_ids, out_weight):
    width = queries.shape[1]
    depth = out_weight.shape[1]
    bf16, f32 = jnp.bfloat16, jnp.float32
    vmem, dma = pltpu.VMEM, pltpu.SemaphoreType.DMA
    table = pltpu.SMEM((BLK_DEV, RAND), jnp.int32)
    anywhere = pl.BlockSpec(memory_space=pl.ANY)
    scalars = pl.BlockSpec(memory_space=pltpu.SMEM)
    out = pl.pallas_call(
        kernel,
        out_shape=jax.ShapeDtypeStruct((BLK_DEV, BLOCK, depth), bf16),
        in_specs=[scalars, scalars, anywhere, anywhere, anywhere],
        out_specs=anywhere,
        scratch_shapes=[
            vmem((EDGE + 1, 2, BLOCK, width), bf16),
            vmem((BLK_DEV, BLOCK, width), bf16),
            vmem((BLK_DEV, BLOCK, width), bf16),
            vmem((BLK_DEV + 2, 2, BLOCK, width), bf16),
            vmem((2, 2, BLOCK, width), bf16),
            vmem((2, 2, BLOCK, width), bf16),
            vmem((2, 2, BLOCK, width), bf16),
            vmem((BLK_DEV, 2, BLOCK, width), bf16),
            vmem((PLANE, SLICE, width), bf16),
            vmem((PLANE, SLICE, width), bf16),
            vmem((RING, SLICE, 128), bf16),
            vmem((SLICE, width), bf16),
            vmem((SLICE, width), bf16),
            vmem((GLOB, 2, BLOCK, width), bf16),
            vmem((BLK_DEV, BLOCK, width), bf16),
            vmem((width, depth), bf16),
            vmem((ENTRIES, BLOCK, width), f32),
            vmem((ENTRIES, BLOCK, width), f32),
            vmem((BLK_DEV, BLOCK, width), f32),
            vmem((BLK_DEV, BLOCK, width), f32),
            vmem((BLK_DEV, BLOCK, width), bf16),
            vmem((BLK_DEV, BLOCK, depth), bf16),
            table, table, table, table,
            pltpu.SMEM((ENTRIES,), jnp.int32),
            pltpu.SMEM((ENTRIES,), jnp.int32),
            dma((8,)),
            dma((3, CHUNKS)), dma((3, CHUNKS)),
            dma((2, CHUNKS)), dma((2, CHUNKS)),
            dma((2, 2, 2)), dma((2, 2, 2)),
            dma((6, CHUNKS)), dma((6, CHUNKS)),
            dma((4,)), dma((4,)),
            dma((2,)), dma((2,)),
            dma((PLANE,)), dma((PLANE,)),
            dma((RING,)), dma((RING,)),
            dma((RING,)), dma((RING,)),
            dma((PLANE,)), dma((PLANE,)),
            pltpu.SemaphoreType.REGULAR,
        ],
        compiler_params=pltpu.CompilerParams(
            collective_id=0, has_side_effects=True, vmem_limit_bytes=60 << 20
        ),
        name="sparse_attention",
    )(
        rand_blocks,
        global_ids,
        queries.reshape(BLK_DEV, BLOCK, width),
        keys_values.reshape(2, BLK_DEV, BLOCK, width),
        out_weight,
    )
    return out.reshape(BLK_DEV * BLOCK, depth)


def solution(mesh):
    placed = (P("seq", None), P(None, "seq", None), P("seq", None), P(), P())
    return jax.shard_map(
        local, mesh=mesh, in_specs=placed, out_specs=P("seq", None), check_vma=False
    )
```

```python
import math

import jax
import jax.numpy as jnp
from jax import lax
from jax.experimental import pallas as pl
from jax.experimental.pallas import tpu as pltpu
from jax.sharding import PartitionSpec as P

HEADS = 8
HEAD_DIM = 128
BLOCK = 128
BLK_DEV = 3
RAND = 3
GLOB = 2
SEG_DEV = 16
SEGS = 16
RING = 8
PLANE = 32
CHUNKS = 2 * BLK_DEV
ENTRIES = BLK_DEV * RAND
EDGE = 10 * BLK_DEV
SLICE = 16
ROOT = 13 * SEG_DEV
SCALE = math.log2(math.e) / math.sqrt(HEAD_DIM)
MESH = pl.DeviceIdType.MESH
OWN, L1, L2, S1, S2, L3 = range(6)


def remote(src, dst, send, recv, device):
    return pltpu.make_async_remote_copy(
        src_ref=src, dst_ref=dst, send_sem=send, recv_sem=recv, device_id=(device,), device_id_type=MESH
    )


def kernel(
    rand_ref, ids_ref, q_hbm, kv_hbm, w_hbm, out_hbm,
    near, l3k, l3v, far, lastk, lastv, stage3, stage4, own, cand, recv1, recv2, sel1, sel2, glob,
    q_ref, w_ref, o_ent, e_ent, o_win, e_win, att, out_ref,
    tab_ls, tab_lo, tab_ss, tab_so, slots, ranks,
    load_sem, long_s, long_r, short_s, short_r, sel_s, sel_r, pair_s, pair_r, tab_s, tab_r, edge_s, edge_r,
    s1, r1, s2, r2, s3, r3, s4, r4, all_in,
):
    me = lax.axis_index("seq")
    core = me % 2
    z = me // 2 % RING
    seg = me // SEG_DEV
    home = me % SEG_DEV
    plane = seg * 2 + core
    other = me + 1 - 2 * core
    go_long = 1 + (RING - 2) * core
    go_short = RING - go_long

    def hop(steps):
        return (z + steps) % RING

    def at(zz, cc):
        return seg * SEG_DEV + zz * 2 + cc

    def at_plane(p):
        return p // 2 * SEG_DEV + z * 2 + p % 2

    loads = [pltpu.make_async_copy(kv_hbm.at[:, j], near.at[j], load_sem.at[j]) for j in range(BLK_DEV)]
    loads += [pltpu.make_async_copy(kv_hbm.at[:, j], own.at[j], load_sem.at[BLK_DEV + j]) for j in range(BLK_DEV)]
    load_q = pltpu.make_async_copy(q_hbm, q_ref, load_sem.at[6])
    load_w = pltpu.make_async_copy(w_hbm, w_ref, load_sem.at[7])
    for copy in loads + [load_q, load_w]:
        copy.start()

    barrier = pltpu.get_barrier_semaphore()

    @pl.loop(1, SEG_DEV)
    def _(i):
        pl.semaphore_signal(
            barrier, inc=1, device_id=(seg * SEG_DEV + (home + i) % SEG_DEV,), device_id_type=MESH
        )

    @pl.when(me != ROOT)
    def _():
        pl.semaphore_wait(barrier, SEG_DEV - 1)

    @pl.when(me == ROOT)
    def _():
        pl.semaphore_wait(barrier, SEG_DEV - 1 + SEGS - 1)

    def mine(shard, q):
        kv, j = q // BLK_DEV, q % BLK_DEV
        if shard == L3:
            return (l3v if kv else l3k).at[j]
        return near.at[shard * BLK_DEV + j, kv]

    def theirs(shard, q):
        kv, j = q // BLK_DEV, q % BLK_DEV
        if shard == L3:
            return far.at[j, kv]
        return near.at[(5 + shard) * BLK_DEV + j, kv]

    longs, shorts = (OWN, L1, L2, L3), (OWN, S1, S2)

    def long(h, q):
        return remote(
            mine(longs[h - 1], q), mine(longs[h], q), long_s.at[h - 1, q], long_r.at[h - 1, q], at(hop(go_long), core)
        )

    def short(h, q):
        return remote(
            mine(shorts[h - 1], q), mine(shorts[h], q), short_s.at[h - 1, q], short_r.at[h - 1, q],
            at(hop(go_short), core),
        )

    def pair(shard, q):
        return remote(mine(shard, q), theirs(shard, q), pair_s.at[shard, q], pair_r.at[shard, q], other)

    for copy in loads[:BLK_DEV]:
        copy.wait()
    for q in range(CHUNKS):
        long(1, q).start()
        short(1, q).start()
    tables = [
        remote(rand_ref, tab_ss, tab_s.at[0], tab_r.at[0], at(hop(go_long), core)),
        remote(rand_ref, tab_ls, tab_s.at[1], tab_r.at[1], at(hop(go_short), core)),
        remote(rand_ref, tab_lo, tab_s.at[2], tab_r.at[2], at(hop(go_long), 1 - core)),
        remote(rand_ref, tab_so, tab_s.at[3], tab_r.at[3], at(hop(go_short), 1 - core)),
    ]
    for copy in tables:
        copy.start()
    for q in range(CHUNKS):
        pair(OWN, q).start()

    head = home == 0

    @pl.when(head & (me != ROOT))
    def _():
        pl.semaphore_signal(barrier, inc=1, device_id=(ROOT,), device_id_type=MESH)

    @pl.when(me == ROOT)
    def _():
        @pl.loop(1, SEGS)
        def _(i):
            pl.semaphore_signal(
                all_in, inc=1, device_id=((seg + i) % SEGS * SEG_DEV,), device_id_type=MESH
            )

    for copy in loads[BLK_DEV:]:
        copy.wait()
    for g in range(GLOB):
        block = ids_ref[g] % BLK_DEV
        for kv in range(2):
            cand[pl.ds((g * 2 + kv) * 8, 8)] = own[block, kv].reshape(8, SLICE, HEADS * HEAD_DIM)

    def code_of(value):
        device = value // BLK_DEV
        delta = (device // 2 + RING - z) % RING
        behind = (delta * core + (RING - delta) * (1 - core)) % RING
        same = jnp.where(device % 2 == core, 1, 0)
        return same, jnp.where(same == 1, behind, (RING - behind) % RING)

    values = [rand_ref[e // RAND, e % RAND] for e in range(ENTRIES)]
    keys = []
    for value in values:
        same, u = code_of(value)
        keys.append(jnp.minimum(u, RING - u) * 32 + u * 2 + same)
    for e in range(ENTRIES):
        ranks[e] = sum(jnp.where(keys[f] < keys[e], 1, 0) for f in range(ENTRIES) if f != e)
    held = [ranks[e] for e in range(ENTRIES)]
    for i in range(ENTRIES):
        slots[i] = sum(jnp.where(held[e] == i, values[e] * 4 + e // RAND, 0) for e in range(ENTRIES))

    @pl.when(head)
    def _():
        @pl.when(me != ROOT)
        def _():
            pl.semaphore_wait(all_in, 1)

        @pl.loop(1, SEG_DEV)
        def _(i):
            pl.semaphore_signal(all_in, inc=1, device_id=(seg * SEG_DEV + i,), device_id_type=MESH)

    @pl.when(home != 0)
    def _():
        pl.semaphore_wait(all_in, 1)

    @pl.loop(1, PLANE)
    def _(i):
        to = (plane + i) % PLANE
        remote(cand.at[to], recv1.at[plane], s1.at[to], r1.at[plane], at_plane(to)).start()

    recv1[plane] = cand[plane]

    which = plane // 16
    owner = ids_ref[0] * (1 - which) + ids_ref[1] * which
    owner = owner // BLK_DEV

    def cols_of(zz):
        return pl.ds(pl.multiple_of(zz * 128, 128), 128)

    def choose_in_plane():
        @pl.loop(1, PLANE)
        def _(i):
            src = (plane + i) % PLANE
            remote(cand.at[src], recv1.at[src], s1.at[src], r1.at[src], other).wait_recv()

        sel1[...] = recv1[owner // SEG_DEV * 2 + owner % 2]

    def scatter_z():
        @pl.loop(1, RING)
        def _(i):
            to = (z + i) % RING
            remote(sel1.at[:, cols_of(to)], recv2.at[z], s2.at[to], r2.at[z], at(to, core)).start()

        recv2[z] = sel1[:, cols_of(z)]

    def choose_in_ring():
        @pl.loop(1, RING)
        def _(i):
            src = (z + i) % RING
            remote(recv2.at[src], recv2.at[src], s2.at[src], r2.at[src], other).wait_recv()

        sel2[:, cols_of(z)] = recv2[owner // 2 % RING]

    def gather_z():
        piece = sel2.at[:, cols_of(z)]

        @pl.loop(1, RING)
        def _(i):
            to = (z + i) % RING
            remote(piece, piece, s3.at[to], r3.at[z], at(to, core)).start()

    def global_slot(p):
        return glob.at[p // 16, p // 8 % 2, pl.ds(pl.multiple_of(p % 8 * SLICE, SLICE), SLICE)]

    def spread_in_plane():
        @pl.loop(1, RING)
        def _(i):
            src = (z + i) % RING
            piece = sel2.at[:, cols_of(src)]
            remote(piece, piece, s3.at[src], r3.at[src], other).wait_recv()

        @pl.loop(1, PLANE)
        def _(i):
            to = (plane + i) % PLANE
            remote(sel2, global_slot(plane), s4.at[to], r4.at[plane], at_plane(to)).start()

        glob[plane // 16, plane // 8 % 2, pl.ds(pl.multiple_of(plane % 8 * SLICE, SLICE), SLICE)] = sel2[...]

    def global_here():
        @pl.loop(1, PLANE)
        def _(i):
            src = (plane + i) % PLANE
            remote(sel2, global_slot(src), s4.at[src], r4.at[src], other).wait_recv()

    def arrive_long(h, q):
        long(h, q).wait_recv()
        if h < 3:
            long(h + 1, q).start()
        pair(longs[h], q).start()

    def arrive_short(h, q):
        short(h, q).wait_recv()
        if h < 2:
            short(h + 1, q).start()
        pair(shorts[h], q).start()

    def wanted(table, source):
        got = 0
        for e in range(ENTRIES):
            value = table[e // RAND, e % RAND]
            got += jnp.where(value // BLK_DEV == source, value % BLK_DEV, 0)
        return got

    def send_sel(third, twin, kv):
        way = go_short if third == 0 else go_long
        stage = (stage3, stage4)[third]
        land = far.at[BLK_DEV + twin, kv] if third == 0 else (lastv if kv else lastk).at[twin]
        to = at(hop(way), core if twin == 0 else 1 - core)
        return remote(stage.at[twin, kv], land, sel_s.at[third, twin, kv], sel_r.at[third, twin, kv], to)

    def columns(head_index):
        return pl.ds(head_index * HEAD_DIM, HEAD_DIM)

    def weigh(queries, keys):
        scores = [
            lax.dot_general(query, key, (((1,), (1,)), ((), ())), preferred_element_type=jnp.float32)
            for query, key in zip(queries, keys)
        ]
        tops = [jnp.max(score, axis=1, keepdims=True) for score in scores]
        probs = [jnp.exp2((score - top) * SCALE) for score, top in zip(scores, tops)]
        totals = [jnp.sum(prob, axis=1, keepdims=True) for prob in probs]
        return [prob.astype(jnp.bfloat16) for prob in probs], tops, totals

    def collect(weighed, values, head_indices, o_ref, e_ref):
        probs, tops, totals = weighed
        outs = [jnp.dot(prob, value, preferred_element_type=jnp.float32) for prob, value in zip(probs, values)]
        for head_index, out, top, total in zip(head_indices, outs, tops, totals):
            o_ref[:, columns(head_index)] = out / total
            e_ref[:, columns(head_index)] = jnp.broadcast_to(top * SCALE + jnp.log2(total), out.shape)

    heads = range(HEADS)

    def entry_parts(i, group):
        packed = slots[i]
        row, value = packed % 4, packed // 4
        same, u = code_of(value)
        j = value % BLK_DEV
        place = jnp.where(u <= 2, u, jnp.where(u == 7, S1, S2))
        is_near = (u <= 2) | (u >= 6)
        near_at = jnp.where(is_near, ((1 - same) * 5 + place) * BLK_DEV + j, 0)
        is_l3 = (u == 3) & (same == 1)
        is_far = ((u == 3) & (same == 0)) | (u == 5)
        far_at = jnp.where(u == 5, BLK_DEV + 1 - same, j)

        def fetch(head_index, kv):
            cols = columns(head_index)
            got = near[near_at, kv, :, cols]
            if group >= 1:
                got = jnp.where(is_l3, (l3v if kv else l3k)[j, :, cols], got)
                got = jnp.where(is_far, far[far_at, kv, :, cols], got)
            if group >= 2:
                got = jnp.where(u == 4, (lastv if kv else lastk)[1 - same, :, cols], got)
            return got

        def first():
            return weigh([q_ref[row, :, columns(h)] for h in heads], [fetch(h, 0) for h in heads])

        def second(weighed):
            collect(weighed, [fetch(h, 1) for h in heads], heads, o_ent.at[i], e_ent.at[i])

        return first, second

    def entry(i, group):
        first, second = entry_parts(i, group)
        second(first())

    def window(b):
        edge_low = (z == 0) & (core == 0)
        edge_high = (z == RING - 1) & (core == 1)
        before = jnp.where(core == 0, (5 + S1) * BLK_DEV + 2, 5 * BLK_DEV + 2)
        before = jnp.where(edge_low, EDGE, before)
        after = jnp.where(core == 0, 5 * BLK_DEV, (5 + S1) * BLK_DEV)
        after = jnp.where(edge_high, EDGE, after)
        places = [before, 0, 1, 2, after][b : b + 3]

        def fetch(head_index, kv):
            cols = columns(head_index)
            return jnp.concatenate(
                [near[p, kv, :, cols] for p in places] + [glob[g, kv, :, cols] for g in range(GLOB)], axis=0
            )

        for some in (heads[: HEADS // 2], heads[HEADS // 2 :]):
            weighed = weigh([q_ref[b, :, columns(h)] for h in some], [fetch(h, 0) for h in some])
            collect(weighed, [fetch(h, 1) for h in some], some, o_win.at[b], e_win.at[b])

    for q in range(CHUNKS):
        arrive_long(1, q)
        arrive_short(1, q)
        if q == 1:
            choose_in_plane()
        if q == 2:
            scatter_z()

    count = SEGS * SEG_DEV
    up = (z == 0) & (core == 1)
    down = (z == RING - 1) & (core == 0)

    def edge(kv, device):
        return remote(
            near.at[S1 * BLK_DEV + 2 * core, kv], near.at[EDGE, kv], edge_s.at[kv], edge_r.at[kv], device
        )

    @pl.when(up)
    def _():
        for kv in range(2):
            edge(kv, (me + SEG_DEV - 1) % count).start()

    @pl.when(down)
    def _():
        for kv in range(2):
            edge(kv, (me + count - SEG_DEV + 1) % count).start()

    for q in range(CHUNKS):
        arrive_long(2, q)
        arrive_short(2, q)
        if q == 0:
            choose_in_ring()
        if q == 1:
            gather_z()
    for q in range(CHUNKS):
        for shard in (OWN, L1, S1, L2, S2):
            pair(shard, q).wait_recv()

    @pl.when((z == 0) & (core == 0) | (z == RING - 1) & (core == 1))
    def _():
        for kv in range(2):
            edge(kv, other).wait_recv()

    for copy, table in zip(tables, (tab_ss, tab_ls, tab_lo, tab_so)):
        copy.wait_recv()
    source = hop(2 * go_long) * 2 + core
    for twin, table in enumerate((tab_ss, tab_so)):
        block = S2 * BLK_DEV + wanted(table, source)
        for kv in range(2):
            stage3[twin, kv] = near[block, kv]
    load_q.wait()
    for kv in range(2):
        for twin in range(2):
            send_sel(0, twin, kv).start()
    spread_in_plane()

    @pl.loop(0, 3)
    def _(i):
        entry(i, 0)

    global_here()
    for b in range(BLK_DEV):
        window(b)

    source = hop(3 * go_short) * 2 + core
    picks = [wanted(table, source) for table in (tab_ls, tab_lo)]
    for q in range(BLK_DEV):
        arrive_long(3, q)
    for twin in range(2):
        stage4[twin, 0] = l3k[picks[twin]]
    for q in range(BLK_DEV):
        pair(L3, q).wait_recv()
    for twin in range(2):
        send_sel(1, twin, 0).start()
    for q in range(BLK_DEV, CHUNKS):
        arrive_long(3, q)
    for twin in range(2):
        stage4[twin, 1] = l3v[picks[twin]]
    for kv in range(2):
        for twin in range(2):
            send_sel(0, twin, kv).wait_recv()
    for twin in range(2):
        send_sel(1, twin, 1).start()
    for q in range(BLK_DEV, CHUNKS):
        pair(L3, q).wait_recv()

    @pl.loop(3, 7)
    def _(i):
        entry(i, 1)

    for q in range(CHUNKS):
        for h in range(1, 4):
            long(h, q).wait_send()
        for h in range(1, 3):
            short(h, q).wait_send()
        for shard in range(6):
            pair(shard, q).wait_send()
    for copy in tables:
        copy.wait_send()

    @pl.when(up | down)
    def _():
        for kv in range(2):
            edge(kv, other).wait_send()

    @pl.loop(1, PLANE)
    def _(i):
        to = (plane + i) % PLANE
        remote(cand.at[to], recv1.at[to], s1.at[to], r1.at[to], other).wait_send()
        remote(sel2, global_slot(plane), s4.at[to], r4.at[to], other).wait_send()

    @pl.loop(1, RING)
    def _(i):
        to = (z + i) % RING
        piece = sel1.at[:, cols_of(to)]
        remote(piece, piece, s2.at[to], r2.at[to], other).wait_send()
        piece = sel2.at[:, cols_of(z)]
        remote(piece, piece, s3.at[to], r3.at[to], other).wait_send()

    load_w.wait()

    for twin in range(2):
        send_sel(1, twin, 0).wait_recv()
    ends = [entry_parts(i, 2) for i in range(7, ENTRIES)]
    halves = [first() for first, _ in ends]
    for twin in range(2):
        send_sel(1, twin, 1).wait_recv()
    for (_, second), half in zip(ends, halves):
        second(half)

    stores = []
    for b in range(BLK_DEV):
        rows = [ranks[b * RAND + r] for r in range(RAND)]
        for head_index in range(HEADS):
            cols = columns(head_index)
            outs = [o_win[b, :, cols]] + [o_ent[r, :, cols] for r in rows]
            logs = [e_win[b, :, cols]] + [e_ent[r, :, cols] for r in rows]
            top = jnp.maximum(jnp.maximum(logs[0], logs[1]), jnp.maximum(logs[2], logs[3]))
            weights = [jnp.exp2(log - top) for log in logs]
            out = sum(w * o for w, o in zip(weights, outs)) / sum(weights)
            att[b, :, cols] = out.astype(jnp.bfloat16)
        out_ref[b] = jnp.dot(att[b], w_ref[...], preferred_element_type=jnp.float32).astype(jnp.bfloat16)
        store = pltpu.make_async_copy(out_ref.at[b], out_hbm.at[b], load_sem.at[b])
        store.start()
        stores.append(store)
    for kv in range(2):
        for twin in range(2):
            send_sel(0, twin, kv).wait_send()
            send_sel(1, twin, kv).wait_send()
    for store in stores:
        store.wait()


def local(queries, keys_values, rand_blocks, global_ids, out_weight):
    width = queries.shape[1]
    depth = out_weight.shape[1]
    bf16, f32 = jnp.bfloat16, jnp.float32
    vmem, dma = pltpu.VMEM, pltpu.SemaphoreType.DMA
    table = pltpu.SMEM((BLK_DEV, RAND), jnp.int32)
    anywhere = pl.BlockSpec(memory_space=pl.ANY)
    scalars = pl.BlockSpec(memory_space=pltpu.SMEM)
    out = pl.pallas_call(
        kernel,
        out_shape=jax.ShapeDtypeStruct((BLK_DEV, BLOCK, depth), bf16),
        in_specs=[scalars, scalars, anywhere, anywhere, anywhere],
        out_specs=anywhere,
        scratch_shapes=[
            vmem((EDGE + 1, 2, BLOCK, width), bf16),
            vmem((BLK_DEV, BLOCK, width), bf16),
            vmem((BLK_DEV, BLOCK, width), bf16),
            vmem((BLK_DEV + 2, 2, BLOCK, width), bf16),
            vmem((2, BLOCK, width), bf16),
            vmem((2, BLOCK, width), bf16),
            vmem((2, 2, BLOCK, width), bf16),
            vmem((2, 2, BLOCK, width), bf16),
            vmem((BLK_DEV, 2, BLOCK, width), bf16),
            vmem((PLANE, SLICE, width), bf16),
            vmem((PLANE, SLICE, width), bf16),
            vmem((RING, SLICE, 128), bf16),
            vmem((SLICE, width), bf16),
            vmem((SLICE, width), bf16),
            vmem((GLOB, 2, BLOCK, width), bf16),
            vmem((BLK_DEV, BLOCK, width), bf16),
            vmem((width, depth), bf16),
            vmem((ENTRIES, BLOCK, width), f32),
            vmem((ENTRIES, BLOCK, width), f32),
            vmem((BLK_DEV, BLOCK, width), f32),
            vmem((BLK_DEV, BLOCK, width), f32),
            vmem((BLK_DEV, BLOCK, width), bf16),
            vmem((BLK_DEV, BLOCK, depth), bf16),
            table, table, table, table,
            pltpu.SMEM((ENTRIES,), jnp.int32),
            pltpu.SMEM((ENTRIES,), jnp.int32),
            dma((8,)),
            dma((3, CHUNKS)), dma((3, CHUNKS)),
            dma((2, CHUNKS)), dma((2, CHUNKS)),
            dma((2, 2, 2)), dma((2, 2, 2)),
            dma((6, CHUNKS)), dma((6, CHUNKS)),
            dma((4,)), dma((4,)),
            dma((2,)), dma((2,)),
            dma((PLANE,)), dma((PLANE,)),
            dma((RING,)), dma((RING,)),
            dma((RING,)), dma((RING,)),
            dma((PLANE,)), dma((PLANE,)),
            pltpu.SemaphoreType.REGULAR,
        ],
        compiler_params=pltpu.CompilerParams(
            collective_id=0, has_side_effects=True, vmem_limit_bytes=60 << 20
        ),
        name="sparse_attention",
    )(
        rand_blocks,
        global_ids,
        queries.reshape(BLK_DEV, BLOCK, width),
        keys_values.reshape(2, BLK_DEV, BLOCK, width),
        out_weight,
    )
    return out.reshape(BLK_DEV * BLOCK, depth)


def solution(mesh):
    placed = (P("seq", None), P(None, "seq", None), P("seq", None), P(), P())
    return jax.shard_map(
        local, mesh=mesh, in_specs=placed, out_specs=P("seq", None), check_vma=False
    )
```

```python
import math

import jax
import jax.numpy as jnp
from jax import lax
from jax.experimental import pallas as pl
from jax.experimental.pallas import tpu as pltpu
from jax.sharding import PartitionSpec as P

HEADS = 8
HEAD_DIM = 128
BLOCK = 128
BLK_DEV = 3
RAND = 3
GLOB = 2
SEG_DEV = 16
SEGS = 16
RING = 8
PLANE = 32
CHUNKS = 2 * BLK_DEV
ENTRIES = BLK_DEV * RAND
EDGE = 10 * BLK_DEV
SLICE = 16
ROOT = 13 * SEG_DEV
SCALE = math.log2(math.e) / math.sqrt(HEAD_DIM)
MESH = pl.DeviceIdType.MESH
OWN, L1, L2, S1, S2, L3 = range(6)


def remote(src, dst, send, recv, device):
    return pltpu.make_async_remote_copy(
        src_ref=src, dst_ref=dst, send_sem=send, recv_sem=recv, device_id=(device,), device_id_type=MESH
    )


def kernel(
    rand_ref, ids_ref, q_hbm, kv_hbm, w_hbm, out_ref,
    near, l3k, l3v, far, lastk, lastv, stage3, stage4, own, cand, recv1, recv2, sel1, sel2, glob,
    q_ref, w_ref, o_ent, e_ent, o_win, e_win, att,
    tab_ls, tab_lo, tab_ss, tab_so, slots, ranks,
    load_sem, long_s, long_r, short_s, short_r, sel_s, sel_r, pair_s, pair_r, tab_s, tab_r, edge_s, edge_r,
    s1, r1, s2, r2, s3, r3, s4, r4, all_in, greet, chain,
):
    me = lax.axis_index("seq")
    core = me % 2
    z = me // 2 % RING
    seg = me // SEG_DEV
    home = me % SEG_DEV
    plane = seg * 2 + core
    other = me + 1 - 2 * core
    go_long = 1 + (RING - 2) * core
    go_short = RING - go_long

    def hop(steps):
        return (z + steps) % RING

    def at(zz, cc):
        return seg * SEG_DEV + zz * 2 + cc

    def at_plane(p):
        return p // 2 * SEG_DEV + z * 2 + p % 2

    loads = [pltpu.make_async_copy(kv_hbm.at[:, j], near.at[j], load_sem.at[j]) for j in range(BLK_DEV)]
    loads += [pltpu.make_async_copy(kv_hbm.at[:, j], own.at[j], load_sem.at[BLK_DEV + j]) for j in range(BLK_DEV)]
    load_q = pltpu.make_async_copy(q_hbm, q_ref, load_sem.at[6])
    load_w = pltpu.make_async_copy(w_hbm, w_ref, load_sem.at[7])
    for copy in loads + [load_q, load_w]:
        copy.start()

    barrier = pltpu.get_barrier_semaphore()

    greeted = [other] + [at(hop(step), cc) for step in (go_long, go_short) for cc in (core, 1 - core)]
    for device in greeted:

        @pl.when((device != ROOT) | (me == ROOT))
        def _(device=device):
            pl.semaphore_signal(barrier, inc=1, device_id=(device,), device_id_type=MESH)

    @pl.when(me != ROOT)
    def _():
        pl.semaphore_wait(barrier, len(greeted))

    for device in greeted:

        @pl.when(device == ROOT)
        def _(device=device):
            pl.semaphore_signal(greet, inc=1, device_id=(device,), device_id_type=MESH)

    @pl.when(me == ROOT)
    def _():
        pl.semaphore_wait(greet, len(greeted))

    def mine(shard, q):
        kv, j = q // BLK_DEV, q % BLK_DEV
        if shard == L3:
            return (l3v if kv else l3k).at[j]
        return near.at[shard * BLK_DEV + j, kv]

    def theirs(shard, q):
        kv, j = q // BLK_DEV, q % BLK_DEV
        if shard == L3:
            return far.at[j, kv]
        return near.at[(5 + shard) * BLK_DEV + j, kv]

    longs, shorts = (OWN, L1, L2, L3), (OWN, S1, S2)

    def long(h, q):
        return remote(
            mine(longs[h - 1], q), mine(longs[h], q), long_s.at[h - 1, q], long_r.at[h - 1, q], at(hop(go_long), core)
        )

    def short(h, q):
        return remote(
            mine(shorts[h - 1], q), mine(shorts[h], q), short_s.at[h - 1, q], short_r.at[h - 1, q],
            at(hop(go_short), core),
        )

    def pair(shard, q):
        return remote(mine(shard, q), theirs(shard, q), pair_s.at[shard, q], pair_r.at[shard, q], other)

    for copy in loads[:BLK_DEV]:
        copy.wait()
    for q in range(CHUNKS):
        long(1, q).start()
        short(1, q).start()
    tables = [
        remote(rand_ref, tab_ss, tab_s.at[0], tab_r.at[0], at(hop(go_long), core)),
        remote(rand_ref, tab_ls, tab_s.at[1], tab_r.at[1], at(hop(go_short), core)),
        remote(rand_ref, tab_lo, tab_s.at[2], tab_r.at[2], at(hop(go_long), 1 - core)),
        remote(rand_ref, tab_so, tab_s.at[3], tab_r.at[3], at(hop(go_short), 1 - core)),
    ]
    for copy in tables:
        copy.start()
    for q in range(CHUNKS):
        pair(OWN, q).start()

    head = home == 0
    middle = RING // 2

    @pl.when(head)
    def _():
        pl.semaphore_wait(chain, 2)

    @pl.when((core == 0) & (z != 0) & (z != middle) & (z != middle + 1))
    def _():
        pl.semaphore_wait(chain, 1)

    @pl.when((core == 0) & (z != 0))
    def _():
        towards = jnp.where(z <= middle, z - 1, hop(1))
        pl.semaphore_signal(chain, inc=1, device_id=(at(towards, 0),), device_id_type=MESH)

    @pl.when(head & (me != ROOT))
    def _():
        pl.semaphore_signal(barrier, inc=1, device_id=(ROOT,), device_id_type=MESH)

    @pl.when(me == ROOT)
    def _():
        pl.semaphore_wait(barrier, SEGS - 1)

        @pl.loop(1, SEGS)
        def _(i):
            pl.semaphore_signal(
                all_in, inc=1, device_id=((seg + i) % SEGS * SEG_DEV,), device_id_type=MESH
            )

    for copy in loads[BLK_DEV:]:
        copy.wait()
    for g in range(GLOB):
        block = ids_ref[g] % BLK_DEV
        for kv in range(2):
            cand[pl.ds((g * 2 + kv) * 8, 8)] = own[block, kv].reshape(8, SLICE, HEADS * HEAD_DIM)

    def code_of(value):
        device = value // BLK_DEV
        delta = (device // 2 + RING - z) % RING
        behind = (delta * core + (RING - delta) * (1 - core)) % RING
        same = jnp.where(device % 2 == core, 1, 0)
        return same, jnp.where(same == 1, behind, (RING - behind) % RING)

    values = [rand_ref[e // RAND, e % RAND] for e in range(ENTRIES)]
    keys = []
    for value in values:
        same, u = code_of(value)
        keys.append(jnp.minimum(u, RING - u) * 32 + u * 2 + same)
    for e in range(ENTRIES):
        ranks[e] = sum(jnp.where(keys[f] < keys[e], 1, 0) for f in range(ENTRIES) if f != e)
    held = [ranks[e] for e in range(ENTRIES)]
    for i in range(ENTRIES):
        slots[i] = sum(jnp.where(held[e] == i, values[e] * 4 + e // RAND, 0) for e in range(ENTRIES))

    @pl.when(head)
    def _():
        @pl.when(me != ROOT)
        def _():
            pl.semaphore_wait(all_in, 1)

        @pl.loop(1, SEG_DEV)
        def _(i):
            pl.semaphore_signal(all_in, inc=1, device_id=(seg * SEG_DEV + i,), device_id_type=MESH)

    @pl.when(home != 0)
    def _():
        pl.semaphore_wait(all_in, 1)

    @pl.loop(1, PLANE)
    def _(i):
        to = (plane + i) % PLANE
        remote(cand.at[to], recv1.at[plane], s1.at[to], r1.at[plane], at_plane(to)).start()

    recv1[plane] = cand[plane]

    which = plane // 16
    owner = ids_ref[0] * (1 - which) + ids_ref[1] * which
    owner = owner // BLK_DEV

    def cols_of(zz):
        return pl.ds(pl.multiple_of(zz * 128, 128), 128)

    def choose_in_plane():
        @pl.loop(1, PLANE)
        def _(i):
            src = (plane + i) % PLANE
            remote(cand.at[src], recv1.at[src], s1.at[src], r1.at[src], other).wait_recv()

        sel1[...] = recv1[owner // SEG_DEV * 2 + owner % 2]

    def scatter_z():
        @pl.loop(1, RING)
        def _(i):
            to = (z + i) % RING
            remote(sel1.at[:, cols_of(to)], recv2.at[z], s2.at[to], r2.at[z], at(to, core)).start()

        recv2[z] = sel1[:, cols_of(z)]

    def choose_in_ring():
        @pl.loop(1, RING)
        def _(i):
            src = (z + i) % RING
            remote(recv2.at[src], recv2.at[src], s2.at[src], r2.at[src], other).wait_recv()

        sel2[:, cols_of(z)] = recv2[owner // 2 % RING]

    def gather_z():
        piece = sel2.at[:, cols_of(z)]

        @pl.loop(1, RING)
        def _(i):
            to = (z + i) % RING
            remote(piece, piece, s3.at[to], r3.at[z], at(to, core)).start()

    def global_slot(p):
        return glob.at[p // 16, p // 8 % 2, pl.ds(pl.multiple_of(p % 8 * SLICE, SLICE), SLICE)]

    def spread_in_plane():
        @pl.loop(1, RING)
        def _(i):
            src = (z + i) % RING
            piece = sel2.at[:, cols_of(src)]
            remote(piece, piece, s3.at[src], r3.at[src], other).wait_recv()

        @pl.loop(1, PLANE)
        def _(i):
            to = (plane + i) % PLANE
            remote(sel2, global_slot(plane), s4.at[to], r4.at[plane], at_plane(to)).start()

        glob[plane // 16, plane // 8 % 2, pl.ds(pl.multiple_of(plane % 8 * SLICE, SLICE), SLICE)] = sel2[...]

    def global_here():
        @pl.loop(1, PLANE)
        def _(i):
            src = (plane + i) % PLANE
            remote(sel2, global_slot(src), s4.at[src], r4.at[src], other).wait_recv()

    def arrive_long(h, q):
        long(h, q).wait_recv()
        if h < 3:
            long(h + 1, q).start()
        pair(longs[h], q).start()

    def arrive_short(h, q):
        short(h, q).wait_recv()
        if h < 2:
            short(h + 1, q).start()
        pair(shorts[h], q).start()

    def wanted(table, source):
        got = 0
        for e in range(ENTRIES):
            value = table[e // RAND, e % RAND]
            got += jnp.where(value // BLK_DEV == source, value % BLK_DEV, 0)
        return got

    def send_sel(third, twin, kv):
        way = go_short if third == 0 else go_long
        stage = (stage3, stage4)[third]
        land = far.at[BLK_DEV + twin, kv] if third == 0 else (lastv if kv else lastk).at[twin]
        to = at(hop(way), core if twin == 0 else 1 - core)
        return remote(stage.at[twin, kv], land, sel_s.at[third, twin, kv], sel_r.at[third, twin, kv], to)

    def columns(head_index):
        return pl.ds(head_index * HEAD_DIM, HEAD_DIM)

    def weigh(queries, keys):
        scores = [
            lax.dot_general(query, key, (((1,), (1,)), ((), ())), preferred_element_type=jnp.float32)
            for query, key in zip(queries, keys)
        ]
        tops = [jnp.max(score, axis=1, keepdims=True) for score in scores]
        probs = [jnp.exp2((score - top) * SCALE) for score, top in zip(scores, tops)]
        totals = [jnp.sum(prob, axis=1, keepdims=True) for prob in probs]
        return [prob.astype(jnp.bfloat16) for prob in probs], tops, totals

    def collect(weighed, values, head_indices, o_ref, e_ref):
        probs, tops, totals = weighed
        outs = [jnp.dot(prob, value, preferred_element_type=jnp.float32) for prob, value in zip(probs, values)]
        for head_index, out, top, total in zip(head_indices, outs, tops, totals):
            o_ref[:, columns(head_index)] = out / total
            e_ref[:, columns(head_index)] = jnp.broadcast_to(top * SCALE + jnp.log2(total), out.shape)

    heads = range(HEADS)

    def entry_parts(i, group):
        packed = slots[i]
        row, value = packed % 4, packed // 4
        same, u = code_of(value)
        j = value % BLK_DEV
        place = jnp.where(u <= 2, u, jnp.where(u == 7, S1, S2))
        is_near = (u <= 2) | (u >= 6)
        near_at = jnp.where(is_near, ((1 - same) * 5 + place) * BLK_DEV + j, 0)
        is_l3 = (u == 3) & (same == 1)
        is_far = ((u == 3) & (same == 0)) | (u == 5)
        far_at = jnp.where(u == 5, BLK_DEV + 1 - same, j)

        def fetch(head_index, kv):
            cols = columns(head_index)
            got = near[near_at, kv, :, cols]
            if group >= 1:
                got = jnp.where(is_l3, (l3v if kv else l3k)[j, :, cols], got)
                got = jnp.where(is_far, far[far_at, kv, :, cols], got)
            if group >= 2:
                got = jnp.where(u == 4, (lastv if kv else lastk)[1 - same, :, cols], got)
            return got

        def first():
            return weigh([q_ref[row, :, columns(h)] for h in heads], [fetch(h, 0) for h in heads])

        def second(weighed):
            collect(weighed, [fetch(h, 1) for h in heads], heads, o_ent.at[i], e_ent.at[i])

        return first, second

    def entry(i, group):
        first, second = entry_parts(i, group)
        second(first())

    def window(b):
        edge_low = (z == 0) & (core == 0)
        edge_high = (z == RING - 1) & (core == 1)
        before = jnp.where(core == 0, (5 + S1) * BLK_DEV + 2, 5 * BLK_DEV + 2)
        before = jnp.where(edge_low, EDGE, before)
        after = jnp.where(core == 0, 5 * BLK_DEV, (5 + S1) * BLK_DEV)
        after = jnp.where(edge_high, EDGE, after)
        places = [before, 0, 1, 2, after][b : b + 3]

        def fetch(head_index, kv):
            cols = columns(head_index)
            return jnp.concatenate(
                [near[p, kv, :, cols] for p in places] + [glob[g, kv, :, cols] for g in range(GLOB)], axis=0
            )

        for some in (heads[: HEADS // 2], heads[HEADS // 2 :]):
            weighed = weigh([q_ref[b, :, columns(h)] for h in some], [fetch(h, 0) for h in some])
            collect(weighed, [fetch(h, 1) for h in some], some, o_win.at[b], e_win.at[b])

    for q in range(CHUNKS):
        arrive_long(1, q)
        arrive_short(1, q)
        if q == 1:
            choose_in_plane()
        if q == 2:
            scatter_z()

    count = SEGS * SEG_DEV
    up = (z == 0) & (core == 1)
    down = (z == RING - 1) & (core == 0)

    def edge(kv, device):
        return remote(
            near.at[S1 * BLK_DEV + 2 * core, kv], near.at[EDGE, kv], edge_s.at[kv], edge_r.at[kv], device
        )

    @pl.when(up)
    def _():
        for kv in range(2):
            edge(kv, (me + SEG_DEV - 1) % count).start()

    @pl.when(down)
    def _():
        for kv in range(2):
            edge(kv, (me + count - SEG_DEV + 1) % count).start()

    for q in range(CHUNKS):
        arrive_long(2, q)
        arrive_short(2, q)
        if q == 0:
            choose_in_ring()
        if q == 1:
            gather_z()
    for q in range(CHUNKS):
        for shard in (OWN, L1, S1, L2, S2):
            pair(shard, q).wait_recv()

    @pl.when((z == 0) & (core == 0) | (z == RING - 1) & (core == 1))
    def _():
        for kv in range(2):
            edge(kv, other).wait_recv()

    for copy, table in zip(tables, (tab_ss, tab_ls, tab_lo, tab_so)):
        copy.wait_recv()
    source = hop(2 * go_long) * 2 + core
    for twin, table in enumerate((tab_ss, tab_so)):
        block = S2 * BLK_DEV + wanted(table, source)
        for kv in range(2):
            stage3[twin, kv] = near[block, kv]
    load_q.wait()
    for kv in range(2):
        for twin in range(2):
            send_sel(0, twin, kv).start()
    spread_in_plane()

    @pl.loop(0, 3)
    def _(i):
        entry(i, 0)

    global_here()
    for b in range(BLK_DEV):
        window(b)

    source = hop(3 * go_short) * 2 + core
    picks = [wanted(table, source) for table in (tab_ls, tab_lo)]
    for q in range(BLK_DEV):
        arrive_long(3, q)
    for twin in range(2):
        stage4[twin, 0] = l3k[picks[twin]]
    for q in range(BLK_DEV):
        pair(L3, q).wait_recv()
    for twin in range(2):
        send_sel(1, twin, 0).start()
    for q in range(BLK_DEV, CHUNKS):
        arrive_long(3, q)
    for twin in range(2):
        stage4[twin, 1] = l3v[picks[twin]]
    for kv in range(2):
        for twin in range(2):
            send_sel(0, twin, kv).wait_recv()
    for twin in range(2):
        send_sel(1, twin, 1).start()
    for q in range(BLK_DEV, CHUNKS):
        pair(L3, q).wait_recv()

    @pl.loop(3, 7)
    def _(i):
        entry(i, 1)

    for q in range(CHUNKS):
        for h in range(1, 4):
            long(h, q).wait_send()
        for h in range(1, 3):
            short(h, q).wait_send()
        for shard in range(6):
            pair(shard, q).wait_send()
    for copy in tables:
        copy.wait_send()

    @pl.when(up | down)
    def _():
        for kv in range(2):
            edge(kv, other).wait_send()

    @pl.loop(1, PLANE)
    def _(i):
        to = (plane + i) % PLANE
        remote(cand.at[to], recv1.at[to], s1.at[to], r1.at[to], other).wait_send()
        remote(sel2, global_slot(plane), s4.at[to], r4.at[to], other).wait_send()

    @pl.loop(1, RING)
    def _(i):
        to = (z + i) % RING
        piece = sel1.at[:, cols_of(to)]
        remote(piece, piece, s2.at[to], r2.at[to], other).wait_send()
        piece = sel2.at[:, cols_of(z)]
        remote(piece, piece, s3.at[to], r3.at[to], other).wait_send()

    load_w.wait()

    for twin in range(2):
        send_sel(1, twin, 0).wait_recv()
    ends = [entry_parts(i, 2) for i in range(7, ENTRIES)]
    halves = [first() for first, _ in ends]
    for twin in range(2):
        send_sel(1, twin, 1).wait_recv()
    for (_, second), half in zip(ends, halves):
        second(half)

    for b in range(BLK_DEV):
        rows = [ranks[b * RAND + r] for r in range(RAND)]
        for head_index in range(HEADS):
            cols = columns(head_index)
            outs = [o_win[b, :, cols]] + [o_ent[r, :, cols] for r in rows]
            logs = [e_win[b, :, cols]] + [e_ent[r, :, cols] for r in rows]
            top = jnp.maximum(jnp.maximum(logs[0], logs[1]), jnp.maximum(logs[2], logs[3]))
            weights = [jnp.exp2(log - top) for log in logs]
            out = sum(w * o for w, o in zip(weights, outs)) / sum(weights)
            att[b, :, cols] = out.astype(jnp.bfloat16)
        out_ref[b] = jnp.dot(att[b], w_ref[...], preferred_element_type=jnp.float32).astype(jnp.bfloat16)
    for kv in range(2):
        for twin in range(2):
            send_sel(0, twin, kv).wait_send()
            send_sel(1, twin, kv).wait_send()


def put_kernel(x_ref, out_ref, sem):
    copy = pltpu.make_async_copy(x_ref, out_ref, sem)
    copy.start()
    copy.wait()


def put(x):
    return pl.pallas_call(
        put_kernel,
        out_shape=jax.ShapeDtypeStruct(x.shape, x.dtype),
        in_specs=[pl.BlockSpec(memory_space=pltpu.VMEM)],
        out_specs=pl.BlockSpec(memory_space=pltpu.HBM),
        scratch_shapes=[pltpu.SemaphoreType.DMA],
        compiler_params=pltpu.CompilerParams(vmem_limit_bytes=4 << 20),
        name="put",
    )(x)


def local(queries, keys_values, rand_blocks, global_ids, out_weight):
    width = queries.shape[1]
    depth = out_weight.shape[1]
    bf16, f32 = jnp.bfloat16, jnp.float32
    vmem, dma = pltpu.VMEM, pltpu.SemaphoreType.DMA
    table = pltpu.SMEM((BLK_DEV, RAND), jnp.int32)
    in_hbm = pl.BlockSpec(memory_space=pltpu.HBM)
    scalars = pl.BlockSpec(memory_space=pltpu.SMEM)
    out = pl.pallas_call(
        kernel,
        out_shape=pltpu.VMEM((BLK_DEV, BLOCK, depth), bf16),
        in_specs=[scalars, scalars, in_hbm, in_hbm, in_hbm],
        out_specs=pl.BlockSpec(memory_space=pltpu.VMEM),
        scratch_shapes=[
            vmem((EDGE + 1, 2, BLOCK, width), bf16),
            vmem((BLK_DEV, BLOCK, width), bf16),
            vmem((BLK_DEV, BLOCK, width), bf16),
            vmem((BLK_DEV + 2, 2, BLOCK, width), bf16),
            vmem((2, BLOCK, width), bf16),
            vmem((2, BLOCK, width), bf16),
            vmem((2, 2, BLOCK, width), bf16),
            vmem((2, 2, BLOCK, width), bf16),
            vmem((BLK_DEV, 2, BLOCK, width), bf16),
            vmem((PLANE, SLICE, width), bf16),
            vmem((PLANE, SLICE, width), bf16),
            vmem((RING, SLICE, 128), bf16),
            vmem((SLICE, width), bf16),
            vmem((SLICE, width), bf16),
            vmem((GLOB, 2, BLOCK, width), bf16),
            vmem((BLK_DEV, BLOCK, width), bf16),
            vmem((width, depth), bf16),
            vmem((ENTRIES, BLOCK, width), f32),
            vmem((ENTRIES, BLOCK, width), f32),
            vmem((BLK_DEV, BLOCK, width), f32),
            vmem((BLK_DEV, BLOCK, width), f32),
            vmem((BLK_DEV, BLOCK, width), bf16),
            table, table, table, table,
            pltpu.SMEM((ENTRIES,), jnp.int32),
            pltpu.SMEM((ENTRIES,), jnp.int32),
            dma((8,)),
            dma((3, CHUNKS)), dma((3, CHUNKS)),
            dma((2, CHUNKS)), dma((2, CHUNKS)),
            dma((2, 2, 2)), dma((2, 2, 2)),
            dma((6, CHUNKS)), dma((6, CHUNKS)),
            dma((4,)), dma((4,)),
            dma((2,)), dma((2,)),
            dma((PLANE,)), dma((PLANE,)),
            dma((RING,)), dma((RING,)),
            dma((RING,)), dma((RING,)),
            dma((PLANE,)), dma((PLANE,)),
            pltpu.SemaphoreType.REGULAR,
            pltpu.SemaphoreType.REGULAR,
            pltpu.SemaphoreType.REGULAR,
        ],
        compiler_params=pltpu.CompilerParams(
            collective_id=0, has_side_effects=True, vmem_limit_bytes=56 << 20
        ),
        name="sparse_attention",
    )(
        rand_blocks,
        global_ids,
        queries.reshape(BLK_DEV, BLOCK, width),
        keys_values.reshape(2, BLK_DEV, BLOCK, width),
        out_weight,
    )
    return put(out.reshape(BLK_DEV * BLOCK, depth))


def solution(mesh):
    placed = (P("seq", None), P(None, "seq", None), P("seq", None), P(), P())
    return jax.shard_map(
        local, mesh=mesh, in_specs=placed, out_specs=P("seq", None), check_vma=False
    )
```

```python
import math

import jax
import jax.numpy as jnp
from jax import lax
from jax.experimental import pallas as pl
from jax.experimental.pallas import tpu as pltpu
from jax.sharding import PartitionSpec as P

HEADS = 8
HEAD_DIM = 128
BLOCK = 128
BLK_DEV = 3
RAND = 3
GLOB = 2
SEG_DEV = 16
SEGS = 16
RING = 8
PLANE = 32
CHUNKS = 2 * BLK_DEV
ENTRIES = BLK_DEV * RAND
EDGE = 10 * BLK_DEV
SLICE = 16
ROOT = 13 * SEG_DEV
SCALE = math.log2(math.e) / math.sqrt(HEAD_DIM)
MESH = pl.DeviceIdType.MESH
OWN, L1, L2, S1, S2, L3 = range(6)


def remote(src, dst, send, recv, device):
    return pltpu.make_async_remote_copy(
        src_ref=src, dst_ref=dst, send_sem=send, recv_sem=recv, device_id=(device,), device_id_type=MESH
    )


def kernel(
    rand_ref, ids_ref, q_hbm, kv_hbm, w_hbm, out_ref,
    near, l3k, l3v, far, lastk, lastv, stage3, stage4, own, cand, recv1, recv2, sel1, piece, sel2, glob,
    q_ref, w_ref, o_ent, e_ent, o_win, e_win, att,
    tab_ls, tab_lo, tab_ss, tab_so, slots, ranks,
    load_sem, long_s, long_r, short_s, short_r, sel_s, sel_r, pair_s, pair_r, tab_s, tab_r, edge_s, edge_r,
    s1, r1, s2, r2, s3, r3, s4, r4, all_in, greet, chain,
):
    me = lax.axis_index("seq")
    core = me % 2
    z = me // 2 % RING
    seg = me // SEG_DEV
    home = me % SEG_DEV
    plane = seg * 2 + core
    other = me + 1 - 2 * core
    go_long = 1 + (RING - 2) * core
    go_short = RING - go_long

    def hop(steps):
        return (z + steps) % RING

    def at(zz, cc):
        return seg * SEG_DEV + zz * 2 + cc

    def at_plane(p):
        return p // 2 * SEG_DEV + z * 2 + p % 2

    loads = [pltpu.make_async_copy(kv_hbm.at[:, j], near.at[j], load_sem.at[j]) for j in range(BLK_DEV)]
    loads += [pltpu.make_async_copy(kv_hbm.at[:, j], own.at[j], load_sem.at[BLK_DEV + j]) for j in range(BLK_DEV)]
    load_q = pltpu.make_async_copy(q_hbm, q_ref, load_sem.at[6])
    load_w = pltpu.make_async_copy(w_hbm, w_ref, load_sem.at[7])
    for copy in loads + [load_q, load_w]:
        copy.start()

    barrier = pltpu.get_barrier_semaphore()

    greeted = [other] + [at(hop(step), cc) for step in (go_long, go_short) for cc in (core, 1 - core)]
    for device in greeted:

        @pl.when((device != ROOT) | (me == ROOT))
        def _(device=device):
            pl.semaphore_signal(barrier, inc=1, device_id=(device,), device_id_type=MESH)

    @pl.when(me != ROOT)
    def _():
        pl.semaphore_wait(barrier, len(greeted))

    for device in greeted:

        @pl.when(device == ROOT)
        def _(device=device):
            pl.semaphore_signal(greet, inc=1, device_id=(device,), device_id_type=MESH)

    @pl.when(me == ROOT)
    def _():
        pl.semaphore_wait(greet, len(greeted))

    def mine(shard, q):
        kv, j = q // BLK_DEV, q % BLK_DEV
        if shard == L3:
            return (l3v if kv else l3k).at[j]
        return near.at[shard * BLK_DEV + j, kv]

    def theirs(shard, q):
        kv, j = q // BLK_DEV, q % BLK_DEV
        if shard == L3:
            return far.at[j, kv]
        return near.at[(5 + shard) * BLK_DEV + j, kv]

    longs, shorts = (OWN, L1, L2, L3), (OWN, S1, S2)

    def long(h, q):
        return remote(
            mine(longs[h - 1], q), mine(longs[h], q), long_s.at[h - 1, q], long_r.at[h - 1, q], at(hop(go_long), core)
        )

    def short(h, q):
        return remote(
            mine(shorts[h - 1], q), mine(shorts[h], q), short_s.at[h - 1, q], short_r.at[h - 1, q],
            at(hop(go_short), core),
        )

    def pair(shard, q):
        return remote(mine(shard, q), theirs(shard, q), pair_s.at[shard, q], pair_r.at[shard, q], other)

    for copy in loads[:BLK_DEV]:
        copy.wait()
    for q in range(CHUNKS):
        long(1, q).start()
        short(1, q).start()
    tables = [
        remote(rand_ref, tab_ss, tab_s.at[0], tab_r.at[0], at(hop(go_long), core)),
        remote(rand_ref, tab_ls, tab_s.at[1], tab_r.at[1], at(hop(go_short), core)),
        remote(rand_ref, tab_lo, tab_s.at[2], tab_r.at[2], at(hop(go_long), 1 - core)),
        remote(rand_ref, tab_so, tab_s.at[3], tab_r.at[3], at(hop(go_short), 1 - core)),
    ]
    for copy in tables:
        copy.start()
    for q in range(CHUNKS):
        pair(OWN, q).start()

    head = home == 0
    middle = RING // 2

    @pl.when(head)
    def _():
        pl.semaphore_wait(chain, 2)

    @pl.when((core == 0) & (z != 0) & (z != middle) & (z != middle + 1))
    def _():
        pl.semaphore_wait(chain, 1)

    @pl.when((core == 0) & (z != 0))
    def _():
        towards = jnp.where(z <= middle, z - 1, hop(1))
        pl.semaphore_signal(chain, inc=1, device_id=(at(towards, 0),), device_id_type=MESH)

    @pl.when(head & (me != ROOT))
    def _():
        pl.semaphore_signal(barrier, inc=1, device_id=(ROOT,), device_id_type=MESH)

    @pl.when(me == ROOT)
    def _():
        pl.semaphore_wait(barrier, SEGS - 1)

        @pl.loop(1, SEGS)
        def _(i):
            pl.semaphore_signal(
                all_in, inc=1, device_id=((seg + i) % SEGS * SEG_DEV,), device_id_type=MESH
            )

    for copy in loads[BLK_DEV:]:
        copy.wait()
    for g in range(GLOB):
        block = ids_ref[g] % BLK_DEV
        for kv in range(2):
            cand[pl.ds((g * 2 + kv) * 8, 8)] = own[block, kv].reshape(8, SLICE, HEADS * HEAD_DIM)

    def code_of(value):
        device = value // BLK_DEV
        delta = (device // 2 + RING - z) % RING
        behind = (delta * core + (RING - delta) * (1 - core)) % RING
        same = jnp.where(device % 2 == core, 1, 0)
        return same, jnp.where(same == 1, behind, (RING - behind) % RING)

    values = [rand_ref[e // RAND, e % RAND] for e in range(ENTRIES)]
    keys = []
    for value in values:
        same, u = code_of(value)
        keys.append(jnp.minimum(u, RING - u) * 32 + u * 2 + same)
    for e in range(ENTRIES):
        ranks[e] = sum(jnp.where(keys[f] < keys[e], 1, 0) for f in range(ENTRIES) if f != e)
    held = [ranks[e] for e in range(ENTRIES)]
    for i in range(ENTRIES):
        slots[i] = sum(jnp.where(held[e] == i, values[e] * 4 + e // RAND, 0) for e in range(ENTRIES))

    @pl.when(head)
    def _():
        @pl.when(me != ROOT)
        def _():
            pl.semaphore_wait(all_in, 1)

        @pl.loop(1, SEG_DEV)
        def _(i):
            pl.semaphore_signal(all_in, inc=1, device_id=(seg * SEG_DEV + i,), device_id_type=MESH)

    @pl.when(home != 0)
    def _():
        pl.semaphore_wait(all_in, 1)

    @pl.loop(1, PLANE)
    def _(i):
        to = (plane + i) % PLANE
        remote(cand.at[to], recv1.at[plane], s1.at[to], r1.at[plane], at_plane(to)).start()

    recv1[plane] = cand[plane]

    which = plane // 16
    owner = ids_ref[0] * (1 - which) + ids_ref[1] * which
    owner = owner // BLK_DEV

    def cols_of(zz):
        return pl.ds(pl.multiple_of(zz * 128, 128), 128)

    def choose_in_plane():
        @pl.loop(1, PLANE)
        def _(i):
            src = (plane + i) % PLANE
            remote(cand.at[src], recv1.at[src], s1.at[src], r1.at[src], other).wait_recv()

        sel1[...] = recv1[owner // SEG_DEV * 2 + owner % 2]

    def scatter_z():
        @pl.loop(1, RING)
        def _(i):
            to = (z + i) % RING
            remote(sel1.at[:, cols_of(to)], recv2.at[z], s2.at[to], r2.at[z], at(to, core)).start()

        recv2[z] = sel1[:, cols_of(z)]

    def choose_in_ring():
        @pl.loop(1, RING)
        def _(i):
            src = (z + i) % RING
            remote(recv2.at[src], recv2.at[src], s2.at[src], r2.at[src], other).wait_recv()

        piece[...] = recv2[owner // 2 % RING]

    def along_x(step):
        return seg // 4 * 4 + (seg + step) % 4

    slot = along_x(3) * 2 + core

    def gather_z():
        @pl.loop(0, RING)
        def _(to):
            there = along_x(1) * SEG_DEV + to * 2 + core
            remote(piece, sel2.at[:, cols_of(z)], s3.at[to], r3.at[z], there).start()

    def global_slot(p):
        return glob.at[p // 16, p // 8 % 2, pl.ds(pl.multiple_of(p % 8 * SLICE, SLICE), SLICE)]

    def spread_in_plane():
        @pl.loop(0, RING)
        def _(src):
            there = sel2.at[:, cols_of(src)]
            remote(there, there, s3.at[src], r3.at[src], other).wait_recv()

        @pl.loop(1, PLANE)
        def _(i):
            to = (plane + i) % PLANE
            remote(sel2, global_slot(slot), s4.at[to], r4.at[slot], at_plane(to)).start()

        glob[slot // 16, slot // 8 % 2, pl.ds(pl.multiple_of(slot % 8 * SLICE, SLICE), SLICE)] = sel2[...]

    def global_here():
        @pl.loop(1, PLANE)
        def _(i):
            src = (slot + i) % PLANE
            remote(sel2, global_slot(src), s4.at[src], r4.at[src], other).wait_recv()

    def arrive_long(h, q):
        long(h, q).wait_recv()
        if h < 3:
            long(h + 1, q).start()
        pair(longs[h], q).start()

    def arrive_short(h, q):
        short(h, q).wait_recv()
        if h < 2:
            short(h + 1, q).start()
        pair(shorts[h], q).start()

    def wanted(table, source):
        got = 0
        for e in range(ENTRIES):
            value = table[e // RAND, e % RAND]
            got += jnp.where(value // BLK_DEV == source, value % BLK_DEV, 0)
        return got

    def send_sel(third, twin, kv):
        way = go_short if third == 0 else go_long
        stage = (stage3, stage4)[third]
        land = far.at[BLK_DEV + twin, kv] if third == 0 else (lastv if kv else lastk).at[twin]
        to = at(hop(way), core if twin == 0 else 1 - core)
        return remote(stage.at[twin, kv], land, sel_s.at[third, twin, kv], sel_r.at[third, twin, kv], to)

    def columns(head_index):
        return pl.ds(head_index * HEAD_DIM, HEAD_DIM)

    def weigh(queries, keys):
        scores = [
            lax.dot_general(query, key, (((1,), (1,)), ((), ())), preferred_element_type=jnp.float32)
            for query, key in zip(queries, keys)
        ]
        tops = [jnp.max(score, axis=1, keepdims=True) for score in scores]
        probs = [jnp.exp2((score - top) * SCALE) for score, top in zip(scores, tops)]
        totals = [jnp.sum(prob, axis=1, keepdims=True) for prob in probs]
        return [prob.astype(jnp.bfloat16) for prob in probs], tops, totals

    def collect(weighed, values, head_indices, o_ref, e_ref):
        probs, tops, totals = weighed
        outs = [jnp.dot(prob, value, preferred_element_type=jnp.float32) for prob, value in zip(probs, values)]
        for head_index, out, top, total in zip(head_indices, outs, tops, totals):
            o_ref[:, columns(head_index)] = out / total
            e_ref[:, columns(head_index)] = jnp.broadcast_to(top * SCALE + jnp.log2(total), out.shape)

    heads = range(HEADS)

    def entry_parts(i, group):
        packed = slots[i]
        row, value = packed % 4, packed // 4
        same, u = code_of(value)
        j = value % BLK_DEV
        place = jnp.where(u <= 2, u, jnp.where(u == 7, S1, S2))
        is_near = (u <= 2) | (u >= 6)
        near_at = jnp.where(is_near, ((1 - same) * 5 + place) * BLK_DEV + j, 0)
        is_l3 = (u == 3) & (same == 1)
        is_far = ((u == 3) & (same == 0)) | (u == 5)
        far_at = jnp.where(u == 5, BLK_DEV + 1 - same, j)

        def fetch(head_index, kv):
            cols = columns(head_index)
            got = near[near_at, kv, :, cols]
            if group >= 1:
                got = jnp.where(is_l3, (l3v if kv else l3k)[j, :, cols], got)
                got = jnp.where(is_far, far[far_at, kv, :, cols], got)
            if group >= 2:
                got = jnp.where(u == 4, (lastv if kv else lastk)[1 - same, :, cols], got)
            return got

        def first():
            return weigh([q_ref[row, :, columns(h)] for h in heads], [fetch(h, 0) for h in heads])

        def second(weighed):
            collect(weighed, [fetch(h, 1) for h in heads], heads, o_ent.at[i], e_ent.at[i])

        return first, second

    def entry(i, group):
        first, second = entry_parts(i, group)
        second(first())

    def window(b):
        edge_low = (z == 0) & (core == 0)
        edge_high = (z == RING - 1) & (core == 1)
        before = jnp.where(core == 0, (5 + S1) * BLK_DEV + 2, 5 * BLK_DEV + 2)
        before = jnp.where(edge_low, EDGE, before)
        after = jnp.where(core == 0, 5 * BLK_DEV, (5 + S1) * BLK_DEV)
        after = jnp.where(edge_high, EDGE, after)
        places = [before, 0, 1, 2, after][b : b + 3]

        def fetch(head_index, kv):
            cols = columns(head_index)
            return jnp.concatenate(
                [near[p, kv, :, cols] for p in places] + [glob[g, kv, :, cols] for g in range(GLOB)], axis=0
            )

        for some in (heads[: HEADS // 2], heads[HEADS // 2 :]):
            weighed = weigh([q_ref[b, :, columns(h)] for h in some], [fetch(h, 0) for h in some])
            collect(weighed, [fetch(h, 1) for h in some], some, o_win.at[b], e_win.at[b])

    for q in range(CHUNKS):
        arrive_long(1, q)
        arrive_short(1, q)
        if q == 1:
            choose_in_plane()
        if q == 2:
            scatter_z()

    count = SEGS * SEG_DEV
    up = (z == 0) & (core == 1)
    down = (z == RING - 1) & (core == 0)

    def edge(kv, device):
        return remote(
            near.at[S1 * BLK_DEV + 2 * core, kv], near.at[EDGE, kv], edge_s.at[kv], edge_r.at[kv], device
        )

    @pl.when(up)
    def _():
        for kv in range(2):
            edge(kv, (me + SEG_DEV - 1) % count).start()

    @pl.when(down)
    def _():
        for kv in range(2):
            edge(kv, (me + count - SEG_DEV + 1) % count).start()

    for q in range(CHUNKS):
        arrive_long(2, q)
        arrive_short(2, q)
        if q == 0:
            choose_in_ring()
        if q == 1:
            gather_z()
        if q == 4:
            spread_in_plane()
    for q in range(CHUNKS):
        for shard in (OWN, L1, S1, L2, S2):
            pair(shard, q).wait_recv()

    @pl.when((z == 0) & (core == 0) | (z == RING - 1) & (core == 1))
    def _():
        for kv in range(2):
            edge(kv, other).wait_recv()

    for copy, table in zip(tables, (tab_ss, tab_ls, tab_lo, tab_so)):
        copy.wait_recv()
    source = hop(2 * go_long) * 2 + core
    for twin, table in enumerate((tab_ss, tab_so)):
        block = S2 * BLK_DEV + wanted(table, source)
        for kv in range(2):
            stage3[twin, kv] = near[block, kv]
    load_q.wait()
    for kv in range(2):
        for twin in range(2):
            send_sel(0, twin, kv).start()

    @pl.loop(0, 3)
    def _(i):
        entry(i, 0)

    global_here()
    for b in range(BLK_DEV):
        window(b)

    source = hop(3 * go_short) * 2 + core
    picks = [wanted(table, source) for table in (tab_ls, tab_lo)]
    for q in range(BLK_DEV):
        arrive_long(3, q)
    for twin in range(2):
        stage4[twin, 0] = l3k[picks[twin]]

    @pl.loop(1, PLANE)
    def _(i):
        to = (plane + i) % PLANE
        remote(cand.at[to], recv1.at[to], s1.at[to], r1.at[to], other).wait_send()
        remote(sel2, global_slot(slot), s4.at[to], r4.at[to], other).wait_send()

    for twin in range(2):
        send_sel(1, twin, 0).start()
    for q in range(BLK_DEV, CHUNKS):
        arrive_long(3, q)
    for twin in range(2):
        stage4[twin, 1] = l3v[picks[twin]]
    for q in range(CHUNKS):
        long(1, q).wait_send()
        short(1, q).wait_send()
        pair(OWN, q).wait_send()
    for twin in range(2):
        send_sel(1, twin, 1).start()
    for q in range(CHUNKS):
        pair(L3, q).wait_recv()
    for kv in range(2):
        for twin in range(2):
            send_sel(0, twin, kv).wait_recv()

    @pl.loop(3, 7)
    def _(i):
        entry(i, 1)

    def merge(outs, logs):
        top = logs[0]
        for log in logs[1:]:
            top = jnp.maximum(top, log)
        weights = [jnp.exp2(log - top) for log in logs]
        total = sum(weights)
        return sum(weight * out for weight, out in zip(weights, outs)), total, top

    for b in range(BLK_DEV):
        rows = [ranks[b * RAND + r] for r in range(RAND)]
        for head_index in range(HEADS):
            cols = columns(head_index)
            outs = [o_win[b, :, cols]] + [jnp.where(r < 7, o_ent[r, :, cols], 0.0) for r in rows]
            logs = [e_win[b, :, cols]] + [jnp.where(r < 7, e_ent[r, :, cols], -jnp.inf) for r in rows]
            out, total, top = merge(outs, logs)
            o_win[b, :, cols] = out / total
            e_win[b, :, cols] = top + jnp.log2(total)

    for q in range(CHUNKS):
        for h in range(2, 4):
            long(h, q).wait_send()
        short(2, q).wait_send()
        for shard in range(1, 6):
            pair(shard, q).wait_send()
    for copy in tables:
        copy.wait_send()

    @pl.when(up | down)
    def _():
        for kv in range(2):
            edge(kv, other).wait_send()

    @pl.loop(1, RING)
    def _(i):
        to = (z + i) % RING
        there = sel1.at[:, cols_of(to)]
        remote(there, there, s2.at[to], r2.at[to], other).wait_send()

    @pl.loop(0, RING)
    def _(to):
        remote(piece, piece, s3.at[to], r3.at[to], other).wait_send()

    load_w.wait()

    for twin in range(2):
        send_sel(1, twin, 0).wait_recv()
    ends = [entry_parts(i, 2) for i in range(7, ENTRIES)]
    halves = [first() for first, _ in ends]
    for twin in range(2):
        send_sel(1, twin, 1).wait_recv()
    for (_, second), half in zip(ends, halves):
        second(half)

    for b in range(BLK_DEV):
        here = [slots[i] % 4 == b for i in range(7, ENTRIES)]
        for head_index in range(HEADS):
            cols = columns(head_index)
            outs = [o_win[b, :, cols]] + [o_ent[i, :, cols] for i in range(7, ENTRIES)]
            logs = [e_win[b, :, cols]] + [
                jnp.where(at_b, e_ent[i, :, cols], -jnp.inf) for i, at_b in zip(range(7, ENTRIES), here)
            ]
            out, total, _ = merge(outs, logs)
            att[pl.ds(b * BLOCK, BLOCK), cols] = (out / total).astype(jnp.bfloat16)
    part = w_ref.shape[1] // 4
    for n in range(4):
        cols = pl.ds(n * part, part)
        out_ref[:, cols] = jnp.dot(att[...], w_ref[:, cols], preferred_element_type=jnp.float32).astype(jnp.bfloat16)
    for kv in range(2):
        for twin in range(2):
            send_sel(0, twin, kv).wait_send()
            send_sel(1, twin, kv).wait_send()


def put_kernel(x_ref, out_ref, sem):
    copy = pltpu.make_async_copy(x_ref, out_ref, sem)
    copy.start()
    copy.wait()


def put(x):
    return pl.pallas_call(
        put_kernel,
        out_shape=jax.ShapeDtypeStruct(x.shape, x.dtype),
        in_specs=[pl.BlockSpec(memory_space=pltpu.VMEM)],
        out_specs=pl.BlockSpec(memory_space=pltpu.HBM),
        scratch_shapes=[pltpu.SemaphoreType.DMA],
        compiler_params=pltpu.CompilerParams(vmem_limit_bytes=4 << 20),
        name="put",
    )(x)


def local(queries, keys_values, rand_blocks, global_ids, out_weight):
    width = queries.shape[1]
    depth = out_weight.shape[1]
    bf16, f32 = jnp.bfloat16, jnp.float32
    vmem, dma = pltpu.VMEM, pltpu.SemaphoreType.DMA
    table = pltpu.SMEM((BLK_DEV, RAND), jnp.int32)
    in_hbm = pl.BlockSpec(memory_space=pltpu.HBM)
    scalars = pl.BlockSpec(memory_space=pltpu.SMEM)
    out = pl.pallas_call(
        kernel,
        out_shape=pltpu.VMEM((BLK_DEV * BLOCK, depth), bf16),
        in_specs=[scalars, scalars, in_hbm, in_hbm, in_hbm],
        out_specs=pl.BlockSpec(memory_space=pltpu.VMEM),
        scratch_shapes=[
            vmem((EDGE + 1, 2, BLOCK, width), bf16),
            vmem((BLK_DEV, BLOCK, width), bf16),
            vmem((BLK_DEV, BLOCK, width), bf16),
            vmem((BLK_DEV + 2, 2, BLOCK, width), bf16),
            vmem((2, BLOCK, width), bf16),
            vmem((2, BLOCK, width), bf16),
            vmem((2, 2, BLOCK, width), bf16),
            vmem((2, 2, BLOCK, width), bf16),
            vmem((BLK_DEV, 2, BLOCK, width), bf16),
            vmem((PLANE, SLICE, width), bf16),
            vmem((PLANE, SLICE, width), bf16),
            vmem((RING, SLICE, 128), bf16),
            vmem((SLICE, width), bf16),
            vmem((SLICE, 128), bf16),
            vmem((SLICE, width), bf16),
            vmem((GLOB, 2, BLOCK, width), bf16),
            vmem((BLK_DEV, BLOCK, width), bf16),
            vmem((width, depth), bf16),
            vmem((ENTRIES, BLOCK, width), f32),
            vmem((ENTRIES, BLOCK, width), f32),
            vmem((BLK_DEV, BLOCK, width), f32),
            vmem((BLK_DEV, BLOCK, width), f32),
            vmem((BLK_DEV * BLOCK, width), bf16),
            table, table, table, table,
            pltpu.SMEM((ENTRIES,), jnp.int32),
            pltpu.SMEM((ENTRIES,), jnp.int32),
            dma((8,)),
            dma((3, CHUNKS)), dma((3, CHUNKS)),
            dma((2, CHUNKS)), dma((2, CHUNKS)),
            dma((2, 2, 2)), dma((2, 2, 2)),
            dma((6, CHUNKS)), dma((6, CHUNKS)),
            dma((4,)), dma((4,)),
            dma((2,)), dma((2,)),
            dma((PLANE,)), dma((PLANE,)),
            dma((RING,)), dma((RING,)),
            dma((RING,)), dma((RING,)),
            dma((PLANE,)), dma((PLANE,)),
            pltpu.SemaphoreType.REGULAR,
            pltpu.SemaphoreType.REGULAR,
            pltpu.SemaphoreType.REGULAR,
        ],
        compiler_params=pltpu.CompilerParams(
            collective_id=0, has_side_effects=True, vmem_limit_bytes=56 << 20
        ),
        name="sparse_attention",
    )(
        rand_blocks,
        global_ids,
        queries.reshape(BLK_DEV, BLOCK, width),
        keys_values.reshape(2, BLK_DEV, BLOCK, width),
        out_weight,
    )
    return put(out)


def solution(mesh):
    placed = (P("seq", None), P(None, "seq", None), P("seq", None), P(), P())
    return jax.shard_map(
        local, mesh=mesh, in_specs=placed, out_specs=P("seq", None), check_vma=False
    )
```

```python
import math

import jax
import jax.numpy as jnp
from jax import lax
from jax.experimental import pallas as pl
from jax.experimental.pallas import tpu as pltpu
from jax.sharding import PartitionSpec as P

HEADS = 8
HEAD_DIM = 128
BLOCK = 128
BLK_DEV = 3
RAND = 3
GLOB = 2
SEG_DEV = 16
SEGS = 16
RING = 8
PLANE = 32
CHUNKS = 2 * BLK_DEV
ENTRIES = BLK_DEV * RAND
EDGE = 10 * BLK_DEV
SLICE = 16
ROOT = 13 * SEG_DEV
SCALE = math.log2(math.e) / math.sqrt(HEAD_DIM)
MESH = pl.DeviceIdType.MESH
OWN, L1, L2, S1, S2, L3 = range(6)


def remote(src, dst, send, recv, device):
    return pltpu.make_async_remote_copy(
        src_ref=src, dst_ref=dst, send_sem=send, recv_sem=recv, device_id=(device,), device_id_type=MESH
    )


def kernel(
    rand_ref, ids_ref, q_hbm, kv_hbm, w_hbm, out_ref,
    near, l3k, l3v, far, lastk, lastv, stage3, stage4, own, cand, recv1, recv2, sel1, piece, sel2, glob,
    q_ref, w_ref, o_ent, e_ent, o_win, e_win, att,
    tab_ls, tab_lo, tab_ss, tab_so, slots, ranks,
    load_sem, long_s, long_r, short_s, short_r, sel_s, sel_r, pair_s, pair_r, tab_s, tab_r, edge_s, edge_r,
    s1, r1, s2, r2, s3, r3, s4, r4, all_in, greet, chain,
):
    me = lax.axis_index("seq")
    core = me % 2
    z = me // 2 % RING
    seg = me // SEG_DEV
    home = me % SEG_DEV
    plane = seg * 2 + core
    other = me + 1 - 2 * core
    go_long = 1 + (RING - 2) * core
    go_short = RING - go_long

    def hop(steps):
        return (z + steps) % RING

    def at(zz, cc):
        return seg * SEG_DEV + zz * 2 + cc

    def at_plane(p):
        return p // 2 * SEG_DEV + z * 2 + p % 2

    loads = [pltpu.make_async_copy(kv_hbm.at[:, j], near.at[j], load_sem.at[j]) for j in range(BLK_DEV)]
    loads += [pltpu.make_async_copy(kv_hbm.at[:, j], own.at[j], load_sem.at[BLK_DEV + j]) for j in range(BLK_DEV)]
    load_q = pltpu.make_async_copy(q_hbm, q_ref, load_sem.at[6])
    load_w = pltpu.make_async_copy(w_hbm, w_ref, load_sem.at[7])
    for copy in loads + [load_q, load_w]:
        copy.start()

    barrier = pltpu.get_barrier_semaphore()

    greeted = [other] + [at(hop(step), cc) for step in (go_long, go_short) for cc in (core, 1 - core)]
    for device in greeted:

        @pl.when((device != ROOT) | (me == ROOT))
        def _(device=device):
            pl.semaphore_signal(barrier, inc=1, device_id=(device,), device_id_type=MESH)

    @pl.when(me != ROOT)
    def _():
        pl.semaphore_wait(barrier, len(greeted))

    for device in greeted:

        @pl.when(device == ROOT)
        def _(device=device):
            pl.semaphore_signal(greet, inc=1, device_id=(device,), device_id_type=MESH)

    @pl.when(me == ROOT)
    def _():
        pl.semaphore_wait(greet, len(greeted))

    def mine(shard, q):
        kv, j = q // BLK_DEV, q % BLK_DEV
        if shard == L3:
            return (l3v if kv else l3k).at[j]
        return near.at[shard * BLK_DEV + j, kv]

    def theirs(shard, q):
        kv, j = q // BLK_DEV, q % BLK_DEV
        if shard == L3:
            return far.at[j, kv]
        return near.at[(5 + shard) * BLK_DEV + j, kv]

    longs, shorts = (OWN, L1, L2, L3), (OWN, S1, S2)

    def long(h, q):
        return remote(
            mine(longs[h - 1], q), mine(longs[h], q), long_s.at[h - 1, q], long_r.at[h - 1, q], at(hop(go_long), core)
        )

    def short(h, q):
        return remote(
            mine(shorts[h - 1], q), mine(shorts[h], q), short_s.at[h - 1, q], short_r.at[h - 1, q],
            at(hop(go_short), core),
        )

    def pair(shard, q):
        return remote(mine(shard, q), theirs(shard, q), pair_s.at[shard, q], pair_r.at[shard, q], other)

    for copy in loads[:BLK_DEV]:
        copy.wait()
    for q in range(CHUNKS):
        long(1, q).start()
        short(1, q).start()
    tables = [
        remote(rand_ref, tab_ss, tab_s.at[0], tab_r.at[0], at(hop(go_long), core)),
        remote(rand_ref, tab_ls, tab_s.at[1], tab_r.at[1], at(hop(go_short), core)),
        remote(rand_ref, tab_lo, tab_s.at[2], tab_r.at[2], at(hop(go_long), 1 - core)),
        remote(rand_ref, tab_so, tab_s.at[3], tab_r.at[3], at(hop(go_short), 1 - core)),
    ]
    for copy in tables:
        copy.start()
    for q in range(CHUNKS):
        pair(OWN, q).start()

    head = home == 0
    middle = RING // 2

    @pl.when(head)
    def _():
        pl.semaphore_wait(chain, 2)

    @pl.when((core == 0) & (z != 0) & (z != middle) & (z != middle + 1))
    def _():
        pl.semaphore_wait(chain, 1)

    @pl.when((core == 0) & (z != 0))
    def _():
        towards = jnp.where(z <= middle, z - 1, hop(1))
        pl.semaphore_signal(chain, inc=1, device_id=(at(towards, 0),), device_id_type=MESH)

    @pl.when(head & (me != ROOT))
    def _():
        pl.semaphore_signal(barrier, inc=1, device_id=(ROOT,), device_id_type=MESH)

    @pl.when(me == ROOT)
    def _():
        pl.semaphore_wait(barrier, SEGS - 1)

        @pl.loop(1, SEGS)
        def _(i):
            pl.semaphore_signal(
                all_in, inc=1, device_id=((seg + i) % SEGS * SEG_DEV,), device_id_type=MESH
            )

    for copy in loads[BLK_DEV:]:
        copy.wait()
    for g in range(GLOB):
        block = ids_ref[g] % BLK_DEV
        for kv in range(2):
            cand[pl.ds((g * 2 + kv) * 8, 8)] = own[block, kv].reshape(8, SLICE, HEADS * HEAD_DIM)

    def code_of(value):
        device = value // BLK_DEV
        delta = (device // 2 + RING - z) % RING
        behind = (delta * core + (RING - delta) * (1 - core)) % RING
        same = jnp.where(device % 2 == core, 1, 0)
        return same, jnp.where(same == 1, behind, (RING - behind) % RING)

    values = [rand_ref[e // RAND, e % RAND] for e in range(ENTRIES)]
    keys = []
    for value in values:
        same, u = code_of(value)
        keys.append(jnp.minimum(u, RING - u) * 32 + u * 2 + same)
    for e in range(ENTRIES):
        ranks[e] = sum(jnp.where(keys[f] < keys[e], 1, 0) for f in range(ENTRIES) if f != e)
    held = [ranks[e] for e in range(ENTRIES)]
    for i in range(ENTRIES):
        slots[i] = sum(jnp.where(held[e] == i, values[e] * 4 + e // RAND, 0) for e in range(ENTRIES))

    @pl.when(head)
    def _():
        @pl.when(me != ROOT)
        def _():
            pl.semaphore_wait(all_in, 1)

        @pl.loop(1, SEG_DEV)
        def _(i):
            pl.semaphore_signal(all_in, inc=1, device_id=(seg * SEG_DEV + i,), device_id_type=MESH)

    @pl.when(home != 0)
    def _():
        pl.semaphore_wait(all_in, 1)

    @pl.loop(1, PLANE)
    def _(i):
        to = (plane + i) % PLANE
        remote(cand.at[to], recv1.at[plane], s1.at[to], r1.at[plane], at_plane(to)).start()

    recv1[plane] = cand[plane]

    which = plane // 16
    owner = ids_ref[0] * (1 - which) + ids_ref[1] * which
    owner = owner // BLK_DEV

    def cols_of(zz):
        return pl.ds(pl.multiple_of(zz * 128, 128), 128)

    def choose_in_plane():
        @pl.loop(1, PLANE)
        def _(i):
            src = (plane + i) % PLANE
            remote(cand.at[src], recv1.at[src], s1.at[src], r1.at[src], other).wait_recv()

        sel1[...] = recv1[owner // SEG_DEV * 2 + owner % 2]

    def scatter_z():
        @pl.loop(1, RING)
        def _(i):
            to = (z + i) % RING
            remote(sel1.at[:, cols_of(to)], recv2.at[z], s2.at[to], r2.at[z], at(to, core)).start()

        recv2[z] = sel1[:, cols_of(z)]

    def choose_in_ring():
        @pl.loop(1, RING)
        def _(i):
            src = (z + i) % RING
            remote(recv2.at[src], recv2.at[src], s2.at[src], r2.at[src], other).wait_recv()

        piece[...] = recv2[owner // 2 % RING]

    def along_x(step):
        return seg // 4 * 4 + (seg + step) % 4

    slot = along_x(3) * 2 + core

    def gather_z():
        @pl.loop(0, RING)
        def _(to):
            there = along_x(1) * SEG_DEV + to * 2 + core
            remote(piece, sel2.at[:, cols_of(z)], s3.at[to], r3.at[z], there).start()

    def global_slot(p):
        return glob.at[p // 16, p // 8 % 2, pl.ds(pl.multiple_of(p % 8 * SLICE, SLICE), SLICE)]

    def spread_in_plane():
        @pl.loop(0, RING)
        def _(src):
            there = sel2.at[:, cols_of(src)]
            remote(there, there, s3.at[src], r3.at[src], other).wait_recv()

        @pl.loop(1, PLANE)
        def _(i):
            to = (plane + i) % PLANE
            remote(sel2, global_slot(slot), s4.at[to], r4.at[slot], at_plane(to)).start()

        glob[slot // 16, slot // 8 % 2, pl.ds(pl.multiple_of(slot % 8 * SLICE, SLICE), SLICE)] = sel2[...]

    def global_here():
        @pl.loop(1, PLANE)
        def _(i):
            src = (slot + i) % PLANE
            remote(sel2, global_slot(src), s4.at[src], r4.at[src], other).wait_recv()

    def arrive_long(h, q):
        long(h, q).wait_recv()
        if h < 3:
            long(h + 1, q).start()
        pair(longs[h], q).start()

    def arrive_short(h, q):
        short(h, q).wait_recv()
        if h < 2:
            short(h + 1, q).start()
        pair(shorts[h], q).start()

    def wanted(table, source):
        got = 0
        for e in range(ENTRIES):
            value = table[e // RAND, e % RAND]
            got += jnp.where(value // BLK_DEV == source, value % BLK_DEV, 0)
        return got

    def send_sel(third, twin, kv):
        way = go_short if third == 0 else go_long
        stage = (stage3, stage4)[third]
        land = far.at[BLK_DEV + twin, kv] if third == 0 else (lastv if kv else lastk).at[twin]
        to = at(hop(way), core if twin == 0 else 1 - core)
        return remote(stage.at[twin, kv], land, sel_s.at[third, twin, kv], sel_r.at[third, twin, kv], to)

    def columns(head_index):
        return pl.ds(head_index * HEAD_DIM, HEAD_DIM)

    def weigh(queries, keys):
        scores = [
            lax.dot_general(query, key, (((1,), (1,)), ((), ())), preferred_element_type=jnp.float32)
            for query, key in zip(queries, keys)
        ]
        tops = [jnp.max(score, axis=1, keepdims=True) for score in scores]
        probs = [jnp.exp2((score - top) * SCALE) for score, top in zip(scores, tops)]
        totals = [jnp.sum(prob, axis=1, keepdims=True) for prob in probs]
        return [prob.astype(jnp.bfloat16) for prob in probs], tops, totals

    def collect(weighed, values, head_indices, o_ref, e_ref):
        probs, tops, totals = weighed
        outs = [jnp.dot(prob, value, preferred_element_type=jnp.float32) for prob, value in zip(probs, values)]
        for head_index, out, top, total in zip(head_indices, outs, tops, totals):
            o_ref[:, columns(head_index)] = out / total
            e_ref[:, columns(head_index)] = jnp.broadcast_to(top * SCALE + jnp.log2(total), out.shape)

    heads = range(HEADS)

    def entry_parts(i, group):
        packed = slots[i]
        row, value = packed % 4, packed // 4
        same, u = code_of(value)
        j = value % BLK_DEV
        place = jnp.where(u <= 2, u, jnp.where(u == 7, S1, S2))
        is_near = (u <= 2) | (u >= 6)
        near_at = jnp.where(is_near, ((1 - same) * 5 + place) * BLK_DEV + j, 0)
        is_l3 = (u == 3) & (same == 1)
        is_far = ((u == 3) & (same == 0)) | (u == 5)
        far_at = jnp.where(u == 5, BLK_DEV + 1 - same, j)

        def fetch(head_index, kv):
            cols = columns(head_index)
            got = near[near_at, kv, :, cols]
            if group >= 1:
                got = jnp.where(is_l3, (l3v if kv else l3k)[j, :, cols], got)
                got = jnp.where(is_far, far[far_at, kv, :, cols], got)
            if group >= 2:
                got = jnp.where(u == 4, (lastv if kv else lastk)[1 - same, :, cols], got)
            return got

        def first():
            return weigh([q_ref[row, :, columns(h)] for h in heads], [fetch(h, 0) for h in heads])

        def second(weighed):
            collect(weighed, [fetch(h, 1) for h in heads], heads, o_ent.at[i], e_ent.at[i])

        return first, second

    def entry(i, group):
        first, second = entry_parts(i, group)
        second(first())

    def window(b):
        edge_low = (z == 0) & (core == 0)
        edge_high = (z == RING - 1) & (core == 1)
        before = jnp.where(core == 0, (5 + S1) * BLK_DEV + 2, 5 * BLK_DEV + 2)
        before = jnp.where(edge_low, EDGE, before)
        after = jnp.where(core == 0, 5 * BLK_DEV, (5 + S1) * BLK_DEV)
        after = jnp.where(edge_high, EDGE, after)
        places = [before, 0, 1, 2, after][b : b + 3]

        def fetch(head_index, kv):
            cols = columns(head_index)
            return jnp.concatenate(
                [near[p, kv, :, cols] for p in places] + [glob[g, kv, :, cols] for g in range(GLOB)], axis=0
            )

        for some in (heads[: HEADS // 2], heads[HEADS // 2 :]):
            weighed = weigh([q_ref[b, :, columns(h)] for h in some], [fetch(h, 0) for h in some])
            collect(weighed, [fetch(h, 1) for h in some], some, o_win.at[b], e_win.at[b])

    for q in range(CHUNKS):
        arrive_long(1, q)
        arrive_short(1, q)
        if q == 1:
            choose_in_plane()
        if q == 2:
            scatter_z()

    count = SEGS * SEG_DEV
    up = (z == 0) & (core == 1)
    down = (z == RING - 1) & (core == 0)

    def edge(kv, device):
        return remote(
            near.at[S1 * BLK_DEV + 2 * core, kv], near.at[EDGE, kv], edge_s.at[kv], edge_r.at[kv], device
        )

    @pl.when(up)
    def _():
        for kv in range(2):
            edge(kv, (me + SEG_DEV - 1) % count).start()

    @pl.when(down)
    def _():
        for kv in range(2):
            edge(kv, (me + count - SEG_DEV + 1) % count).start()

    for q in range(CHUNKS):
        arrive_long(2, q)
        arrive_short(2, q)
        if q == 0:
            choose_in_ring()
        if q == 1:
            gather_z()
        if q == 4:
            spread_in_plane()
    for q in range(CHUNKS):
        for shard in (OWN, L1, S1, L2, S2):
            pair(shard, q).wait_recv()

    @pl.when((z == 0) & (core == 0) | (z == RING - 1) & (core == 1))
    def _():
        for kv in range(2):
            edge(kv, other).wait_recv()

    for copy, table in zip(tables, (tab_ss, tab_ls, tab_lo, tab_so)):
        copy.wait_recv()
    source = hop(2 * go_long) * 2 + core
    for twin, table in enumerate((tab_ss, tab_so)):
        block = S2 * BLK_DEV + wanted(table, source)
        for kv in range(2):
            stage3[twin, kv] = near[block, kv]
    load_q.wait()
    for kv in range(2):
        for twin in range(2):
            send_sel(0, twin, kv).start()

    @pl.loop(0, 3)
    def _(i):
        entry(i, 0)

    source = hop(3 * go_short) * 2 + core
    picks = [wanted(table, source) for table in (tab_ls, tab_lo)]
    for q in range(BLK_DEV):
        arrive_long(3, q)
    for twin in range(2):
        stage4[twin, 0] = l3k[picks[twin]]

    @pl.loop(1, PLANE)
    def _(i):
        to = (plane + i) % PLANE
        remote(cand.at[to], recv1.at[to], s1.at[to], r1.at[to], other).wait_send()
        remote(sel2, global_slot(slot), s4.at[to], r4.at[to], other).wait_send()

    for twin in range(2):
        send_sel(1, twin, 0).start()
    global_here()
    window(0)
    window(1)
    arrive_long(3, BLK_DEV)
    window(2)
    for q in range(BLK_DEV + 1, CHUNKS):
        arrive_long(3, q)
    for twin in range(2):
        stage4[twin, 1] = l3v[picks[twin]]
    for q in range(CHUNKS):
        long(1, q).wait_send()
        short(1, q).wait_send()
        pair(OWN, q).wait_send()
    for twin in range(2):
        send_sel(1, twin, 1).start()
    for q in range(CHUNKS):
        pair(L3, q).wait_recv()
    for kv in range(2):
        for twin in range(2):
            send_sel(0, twin, kv).wait_recv()

    @pl.loop(3, 7)
    def _(i):
        entry(i, 1)

    def merge(outs, logs):
        top = logs[0]
        for log in logs[1:]:
            top = jnp.maximum(top, log)
        weights = [jnp.exp2(log - top) for log in logs]
        total = sum(weights)
        return sum(weight * out for weight, out in zip(weights, outs)), total, top

    for b in range(BLK_DEV):
        rows = [ranks[b * RAND + r] for r in range(RAND)]
        for head_index in range(HEADS):
            cols = columns(head_index)
            outs = [o_win[b, :, cols]] + [jnp.where(r < 7, o_ent[r, :, cols], 0.0) for r in rows]
            logs = [e_win[b, :, cols]] + [jnp.where(r < 7, e_ent[r, :, cols], -jnp.inf) for r in rows]
            out, total, top = merge(outs, logs)
            o_win[b, :, cols] = out / total
            e_win[b, :, cols] = top + jnp.log2(total)

    for q in range(CHUNKS):
        for h in range(2, 4):
            long(h, q).wait_send()
        short(2, q).wait_send()
        for shard in range(1, 6):
            pair(shard, q).wait_send()
    for copy in tables:
        copy.wait_send()

    @pl.when(up | down)
    def _():
        for kv in range(2):
            edge(kv, other).wait_send()

    @pl.loop(1, RING)
    def _(i):
        to = (z + i) % RING
        there = sel1.at[:, cols_of(to)]
        remote(there, there, s2.at[to], r2.at[to], other).wait_send()

    @pl.loop(0, RING)
    def _(to):
        remote(piece, piece, s3.at[to], r3.at[to], other).wait_send()

    load_w.wait()

    for twin in range(2):
        send_sel(1, twin, 0).wait_recv()
    ends = [entry_parts(i, 2) for i in range(7, ENTRIES)]
    halves = [first() for first, _ in ends]
    for twin in range(2):
        send_sel(1, twin, 1).wait_recv()
    for (_, second), half in zip(ends, halves):
        second(half)

    for b in range(BLK_DEV):
        here = [slots[i] % 4 == b for i in range(7, ENTRIES)]
        for head_index in range(HEADS):
            cols = columns(head_index)
            outs = [o_win[b, :, cols]] + [o_ent[i, :, cols] for i in range(7, ENTRIES)]
            logs = [e_win[b, :, cols]] + [
                jnp.where(at_b, e_ent[i, :, cols], -jnp.inf) for i, at_b in zip(range(7, ENTRIES), here)
            ]
            out, total, _ = merge(outs, logs)
            att[pl.ds(b * BLOCK, BLOCK), cols] = (out / total).astype(jnp.bfloat16)
    part = w_ref.shape[1] // 4
    for n in range(4):
        cols = pl.ds(n * part, part)
        out_ref[:, cols] = jnp.dot(att[...], w_ref[:, cols], preferred_element_type=jnp.float32).astype(jnp.bfloat16)
    for kv in range(2):
        for twin in range(2):
            send_sel(0, twin, kv).wait_send()
            send_sel(1, twin, kv).wait_send()


def put_kernel(x_ref, out_ref, sem):
    copy = pltpu.make_async_copy(x_ref, out_ref, sem)
    copy.start()
    copy.wait()


def put(x):
    return pl.pallas_call(
        put_kernel,
        out_shape=jax.ShapeDtypeStruct(x.shape, x.dtype),
        in_specs=[pl.BlockSpec(memory_space=pltpu.VMEM)],
        out_specs=pl.BlockSpec(memory_space=pltpu.HBM),
        scratch_shapes=[pltpu.SemaphoreType.DMA],
        compiler_params=pltpu.CompilerParams(vmem_limit_bytes=4 << 20),
        name="put",
    )(x)


def local(queries, keys_values, rand_blocks, global_ids, out_weight):
    width = queries.shape[1]
    depth = out_weight.shape[1]
    bf16, f32 = jnp.bfloat16, jnp.float32
    vmem, dma = pltpu.VMEM, pltpu.SemaphoreType.DMA
    table = pltpu.SMEM((BLK_DEV, RAND), jnp.int32)
    in_hbm = pl.BlockSpec(memory_space=pltpu.HBM)
    scalars = pl.BlockSpec(memory_space=pltpu.SMEM)
    out = pl.pallas_call(
        kernel,
        out_shape=pltpu.VMEM((BLK_DEV * BLOCK, depth), bf16),
        in_specs=[scalars, scalars, in_hbm, in_hbm, in_hbm],
        out_specs=pl.BlockSpec(memory_space=pltpu.VMEM),
        scratch_shapes=[
            vmem((EDGE + 1, 2, BLOCK, width), bf16),
            vmem((BLK_DEV, BLOCK, width), bf16),
            vmem((BLK_DEV, BLOCK, width), bf16),
            vmem((BLK_DEV + 2, 2, BLOCK, width), bf16),
            vmem((2, BLOCK, width), bf16),
            vmem((2, BLOCK, width), bf16),
            vmem((2, 2, BLOCK, width), bf16),
            vmem((2, 2, BLOCK, width), bf16),
            vmem((BLK_DEV, 2, BLOCK, width), bf16),
            vmem((PLANE, SLICE, width), bf16),
            vmem((PLANE, SLICE, width), bf16),
            vmem((RING, SLICE, 128), bf16),
            vmem((SLICE, width), bf16),
            vmem((SLICE, 128), bf16),
            vmem((SLICE, width), bf16),
            vmem((GLOB, 2, BLOCK, width), bf16),
            vmem((BLK_DEV, BLOCK, width), bf16),
            vmem((width, depth), bf16),
            vmem((ENTRIES, BLOCK, width), f32),
            vmem((ENTRIES, BLOCK, width), f32),
            vmem((BLK_DEV, BLOCK, width), f32),
            vmem((BLK_DEV, BLOCK, width), f32),
            vmem((BLK_DEV * BLOCK, width), bf16),
            table, table, table, table,
            pltpu.SMEM((ENTRIES,), jnp.int32),
            pltpu.SMEM((ENTRIES,), jnp.int32),
            dma((8,)),
            dma((3, CHUNKS)), dma((3, CHUNKS)),
            dma((2, CHUNKS)), dma((2, CHUNKS)),
            dma((2, 2, 2)), dma((2, 2, 2)),
            dma((6, CHUNKS)), dma((6, CHUNKS)),
            dma((4,)), dma((4,)),
            dma((2,)), dma((2,)),
            dma((PLANE,)), dma((PLANE,)),
            dma((RING,)), dma((RING,)),
            dma((RING,)), dma((RING,)),
            dma((PLANE,)), dma((PLANE,)),
            pltpu.SemaphoreType.REGULAR,
            pltpu.SemaphoreType.REGULAR,
            pltpu.SemaphoreType.REGULAR,
        ],
        compiler_params=pltpu.CompilerParams(
            collective_id=0, has_side_effects=True, vmem_limit_bytes=56 << 20
        ),
        name="sparse_attention",
    )(
        rand_blocks,
        global_ids,
        queries.reshape(BLK_DEV, BLOCK, width),
        keys_values.reshape(2, BLK_DEV, BLOCK, width),
        out_weight,
    )
    return put(out)


def solution(mesh):
    placed = (P("seq", None), P(None, "seq", None), P("seq", None), P(), P())
    return jax.shard_map(
        local, mesh=mesh, in_specs=placed, out_specs=P("seq", None), check_vma=False
    )
```

```python
import math

import jax
import jax.numpy as jnp
from jax import lax
from jax.experimental import pallas as pl
from jax.experimental.pallas import tpu as pltpu
from jax.sharding import PartitionSpec as P

HEADS = 8
HEAD_DIM = 128
BLOCK = 128
BLK_DEV = 3
RAND = 3
GLOB = 2
SEG_DEV = 16
SEGS = 16
RING = 8
PLANE = 32
CHUNKS = 2 * BLK_DEV
ENTRIES = BLK_DEV * RAND
EDGE = 10 * BLK_DEV
SLICE = 16
ROOT = 13 * SEG_DEV
SCALE = math.log2(math.e) / math.sqrt(HEAD_DIM)
MESH = pl.DeviceIdType.MESH
OWN, L1, L2, S1, S2, L3 = range(6)


def remote(src, dst, send, recv, device):
    return pltpu.make_async_remote_copy(
        src_ref=src, dst_ref=dst, send_sem=send, recv_sem=recv, device_id=(device,), device_id_type=MESH
    )


def kernel(
    rand_ref, ids_ref, q_hbm, kv_hbm, w_hbm, out_ref,
    near, l3k, l3v, far, lastk, lastv, stage3, stage4, own, cand, recv1, recv2, sel1, piece, sel2, glob,
    q_ref, w_ref, o_ent, e_ent, o_win, e_win, att,
    tab_ls, tab_lo, tab_ss, tab_so, slots, ranks,
    load_sem, long_s, long_r, short_s, short_r, sel_s, sel_r, pair_s, pair_r, tab_s, tab_r, edge_s, edge_r,
    s1, r1, s2, r2, s3, r3, s4, r4, all_in, greet, chain,
):
    me = lax.axis_index("seq")
    core = me % 2
    z = me // 2 % RING
    seg = me // SEG_DEV
    home = me % SEG_DEV
    plane = seg * 2 + core
    other = me + 1 - 2 * core
    go_long = 1 + (RING - 2) * core
    go_short = RING - go_long

    def hop(steps):
        return (z + steps) % RING

    def at(zz, cc):
        return seg * SEG_DEV + zz * 2 + cc

    def at_plane(p):
        return p // 2 * SEG_DEV + z * 2 + p % 2

    loads = [pltpu.make_async_copy(kv_hbm.at[:, j], near.at[j], load_sem.at[j]) for j in range(BLK_DEV)]
    loads += [pltpu.make_async_copy(kv_hbm.at[:, j], own.at[j], load_sem.at[BLK_DEV + j]) for j in range(BLK_DEV)]
    load_q = pltpu.make_async_copy(q_hbm, q_ref, load_sem.at[6])
    load_w = pltpu.make_async_copy(w_hbm, w_ref, load_sem.at[7])
    for copy in loads + [load_q, load_w]:
        copy.start()

    barrier = pltpu.get_barrier_semaphore()

    greeted = [other] + [at(hop(step), cc) for step in (go_long, go_short) for cc in (core, 1 - core)]
    for device in greeted:

        @pl.when((device != ROOT) | (me == ROOT))
        def _(device=device):
            pl.semaphore_signal(barrier, inc=1, device_id=(device,), device_id_type=MESH)

    @pl.when(me != ROOT)
    def _():
        pl.semaphore_wait(barrier, len(greeted))

    for device in greeted:

        @pl.when(device == ROOT)
        def _(device=device):
            pl.semaphore_signal(greet, inc=1, device_id=(device,), device_id_type=MESH)

    @pl.when(me == ROOT)
    def _():
        pl.semaphore_wait(greet, len(greeted))

    def mine(shard, q):
        kv, j = q // BLK_DEV, q % BLK_DEV
        if shard == L3:
            return (l3v if kv else l3k).at[j]
        return near.at[shard * BLK_DEV + j, kv]

    def theirs(shard, q):
        kv, j = q // BLK_DEV, q % BLK_DEV
        if shard == L3:
            return far.at[j, kv]
        return near.at[(5 + shard) * BLK_DEV + j, kv]

    longs, shorts = (OWN, L1, L2, L3), (OWN, S1, S2)

    def long(h, q):
        return remote(
            mine(longs[h - 1], q), mine(longs[h], q), long_s.at[h - 1, q], long_r.at[h - 1, q], at(hop(go_long), core)
        )

    def short(h, q):
        return remote(
            mine(shorts[h - 1], q), mine(shorts[h], q), short_s.at[h - 1, q], short_r.at[h - 1, q],
            at(hop(go_short), core),
        )

    def pair(shard, q):
        return remote(mine(shard, q), theirs(shard, q), pair_s.at[shard, q], pair_r.at[shard, q], other)

    for copy in loads[:BLK_DEV]:
        copy.wait()
    for q in range(CHUNKS):
        long(1, q).start()
        short(1, q).start()
    tables = [
        remote(rand_ref, tab_ss, tab_s.at[0], tab_r.at[0], at(hop(go_long), core)),
        remote(rand_ref, tab_ls, tab_s.at[1], tab_r.at[1], at(hop(go_short), core)),
        remote(rand_ref, tab_lo, tab_s.at[2], tab_r.at[2], at(hop(go_long), 1 - core)),
        remote(rand_ref, tab_so, tab_s.at[3], tab_r.at[3], at(hop(go_short), 1 - core)),
    ]
    for copy in tables:
        copy.start()
    for q in range(CHUNKS):
        pair(OWN, q).start()

    head = home == 0
    middle = RING // 2

    @pl.when(head)
    def _():
        pl.semaphore_wait(chain, 2)

    @pl.when((core == 0) & (z != 0) & (z != middle) & (z != middle + 1))
    def _():
        pl.semaphore_wait(chain, 1)

    @pl.when((core == 0) & (z != 0))
    def _():
        towards = jnp.where(z <= middle, z - 1, hop(1))
        pl.semaphore_signal(chain, inc=1, device_id=(at(towards, 0),), device_id_type=MESH)

    @pl.when(head & (me != ROOT))
    def _():
        pl.semaphore_signal(barrier, inc=1, device_id=(ROOT,), device_id_type=MESH)

    @pl.when(me == ROOT)
    def _():
        pl.semaphore_wait(barrier, SEGS - 1)

        @pl.loop(1, SEGS)
        def _(i):
            pl.semaphore_signal(
                all_in, inc=1, device_id=((seg + i) % SEGS * SEG_DEV,), device_id_type=MESH
            )

    for copy in loads[BLK_DEV:]:
        copy.wait()
    for g in range(GLOB):
        block = ids_ref[g] % BLK_DEV
        for kv in range(2):
            cand[pl.ds((g * 2 + kv) * 8, 8)] = own[block, kv].reshape(8, SLICE, HEADS * HEAD_DIM)

    def code_of(value):
        device = value // BLK_DEV
        delta = (device // 2 + RING - z) % RING
        behind = (delta * core + (RING - delta) * (1 - core)) % RING
        same = jnp.where(device % 2 == core, 1, 0)
        return same, jnp.where(same == 1, behind, (RING - behind) % RING)

    values = [rand_ref[e // RAND, e % RAND] for e in range(ENTRIES)]
    keys = []
    for value in values:
        same, u = code_of(value)
        keys.append(jnp.minimum(u, RING - u) * 32 + u * 2 + same)
    for e in range(ENTRIES):
        ranks[e] = sum(jnp.where(keys[f] < keys[e], 1, 0) for f in range(ENTRIES) if f != e)
    held = [ranks[e] for e in range(ENTRIES)]
    for i in range(ENTRIES):
        slots[i] = sum(jnp.where(held[e] == i, values[e] * 4 + e // RAND, 0) for e in range(ENTRIES))

    @pl.when(head)
    def _():
        @pl.when(me != ROOT)
        def _():
            pl.semaphore_wait(all_in, 1)

        @pl.loop(1, SEG_DEV)
        def _(i):
            pl.semaphore_signal(all_in, inc=1, device_id=(seg * SEG_DEV + i,), device_id_type=MESH)

    @pl.when(home != 0)
    def _():
        pl.semaphore_wait(all_in, 1)

    @pl.loop(1, PLANE)
    def _(i):
        to = (plane + i) % PLANE
        remote(cand.at[to], recv1.at[plane], s1.at[to], r1.at[plane], at_plane(to)).start()

    recv1[plane] = cand[plane]

    which = plane // 16
    owner = ids_ref[0] * (1 - which) + ids_ref[1] * which
    owner = owner // BLK_DEV

    def cols_of(zz):
        return pl.ds(pl.multiple_of(zz * 128, 128), 128)

    def choose_in_plane():
        @pl.loop(1, PLANE)
        def _(i):
            src = (plane + i) % PLANE
            remote(cand.at[src], recv1.at[src], s1.at[src], r1.at[src], other).wait_recv()

        sel1[...] = recv1[owner // SEG_DEV * 2 + owner % 2]

    def along_x(step):
        return seg // 4 * 4 + (seg + step) % 4

    def scatter_z():
        @pl.loop(0, RING)
        def _(to):
            there = along_x(1) * SEG_DEV + to * 2 + core
            remote(sel1.at[:, cols_of(to)], recv2.at[z], s2.at[to], r2.at[z], there).start()

    def choose_in_ring():
        @pl.loop(0, RING)
        def _(src):
            remote(recv2.at[src], recv2.at[src], s2.at[src], r2.at[src], other).wait_recv()

        piece[...] = recv2[owner // 2 % RING]

    slot = along_x(2) * 2 + core

    def gather_z():
        @pl.loop(0, RING)
        def _(to):
            there = along_x(1) * SEG_DEV + to * 2 + core
            remote(piece, sel2.at[:, cols_of(z)], s3.at[to], r3.at[z], there).start()

    def global_slot(p):
        return glob.at[p // 16, p // 8 % 2, pl.ds(pl.multiple_of(p % 8 * SLICE, SLICE), SLICE)]

    def spread_in_plane():
        @pl.loop(0, RING)
        def _(src):
            there = sel2.at[:, cols_of(src)]
            remote(there, there, s3.at[src], r3.at[src], other).wait_recv()

        @pl.loop(1, PLANE)
        def _(i):
            to = (plane + i) % PLANE
            remote(sel2, global_slot(slot), s4.at[to], r4.at[slot], at_plane(to)).start()

        glob[slot // 16, slot // 8 % 2, pl.ds(pl.multiple_of(slot % 8 * SLICE, SLICE), SLICE)] = sel2[...]

    def global_here():
        @pl.loop(1, PLANE)
        def _(i):
            src = (slot + i) % PLANE
            remote(sel2, global_slot(src), s4.at[src], r4.at[src], other).wait_recv()

    def arrive_long(h, q):
        long(h, q).wait_recv()
        if h < 3:
            long(h + 1, q).start()
        pair(longs[h], q).start()

    def arrive_short(h, q):
        short(h, q).wait_recv()
        if h < 2:
            short(h + 1, q).start()
        pair(shorts[h], q).start()

    def wanted(table, source):
        got = 0
        for e in range(ENTRIES):
            value = table[e // RAND, e % RAND]
            got += jnp.where(value // BLK_DEV == source, value % BLK_DEV, 0)
        return got

    def send_sel(third, twin, kv):
        way = go_short if third == 0 else go_long
        stage = (stage3, stage4)[third]
        land = far.at[BLK_DEV + twin, kv] if third == 0 else (lastv if kv else lastk).at[twin]
        to = at(hop(way), core if twin == 0 else 1 - core)
        return remote(stage.at[twin, kv], land, sel_s.at[third, twin, kv], sel_r.at[third, twin, kv], to)

    def columns(head_index):
        return pl.ds(head_index * HEAD_DIM, HEAD_DIM)

    def weigh(queries, keys):
        scores = [
            lax.dot_general(query, key, (((1,), (1,)), ((), ())), preferred_element_type=jnp.float32)
            for query, key in zip(queries, keys)
        ]
        tops = [jnp.max(score, axis=1, keepdims=True) for score in scores]
        probs = [jnp.exp2((score - top) * SCALE) for score, top in zip(scores, tops)]
        totals = [jnp.sum(prob, axis=1, keepdims=True) for prob in probs]
        return [prob.astype(jnp.bfloat16) for prob in probs], tops, totals

    def collect(weighed, values, head_indices, o_ref, e_ref):
        probs, tops, totals = weighed
        outs = [jnp.dot(prob, value, preferred_element_type=jnp.float32) for prob, value in zip(probs, values)]
        for head_index, out, top, total in zip(head_indices, outs, tops, totals):
            o_ref[:, columns(head_index)] = out / total
            e_ref[:, columns(head_index)] = jnp.broadcast_to(top * SCALE + jnp.log2(total), out.shape)

    heads = range(HEADS)

    def entry_parts(i, group):
        packed = slots[i]
        row, value = packed % 4, packed // 4
        same, u = code_of(value)
        j = value % BLK_DEV
        place = jnp.where(u <= 2, u, jnp.where(u == 7, S1, S2))
        is_near = (u <= 2) | (u >= 6)
        near_at = jnp.where(is_near, ((1 - same) * 5 + place) * BLK_DEV + j, 0)
        is_l3 = (u == 3) & (same == 1)
        is_far = ((u == 3) & (same == 0)) | (u == 5)
        far_at = jnp.where(u == 5, BLK_DEV + 1 - same, j)

        def fetch(head_index, kv):
            cols = columns(head_index)
            got = near[near_at, kv, :, cols]
            if group >= 1:
                got = jnp.where(is_l3, (l3v if kv else l3k)[j, :, cols], got)
                got = jnp.where(is_far, far[far_at, kv, :, cols], got)
            if group >= 2:
                got = jnp.where(u == 4, (lastv if kv else lastk)[1 - same, :, cols], got)
            return got

        def first():
            return weigh([q_ref[row, :, columns(h)] for h in heads], [fetch(h, 0) for h in heads])

        def second(weighed):
            collect(weighed, [fetch(h, 1) for h in heads], heads, o_ent.at[i], e_ent.at[i])

        return first, second

    def entry(i, group):
        first, second = entry_parts(i, group)
        second(first())

    def window(b):
        edge_low = (z == 0) & (core == 0)
        edge_high = (z == RING - 1) & (core == 1)
        before = jnp.where(core == 0, (5 + S1) * BLK_DEV + 2, 5 * BLK_DEV + 2)
        before = jnp.where(edge_low, EDGE, before)
        after = jnp.where(core == 0, 5 * BLK_DEV, (5 + S1) * BLK_DEV)
        after = jnp.where(edge_high, EDGE, after)
        places = [before, 0, 1, 2, after][b : b + 3]

        def fetch(head_index, kv):
            cols = columns(head_index)
            return jnp.concatenate(
                [near[p, kv, :, cols] for p in places] + [glob[g, kv, :, cols] for g in range(GLOB)], axis=0
            )

        for some in (heads[: HEADS // 2], heads[HEADS // 2 :]):
            weighed = weigh([q_ref[b, :, columns(h)] for h in some], [fetch(h, 0) for h in some])
            collect(weighed, [fetch(h, 1) for h in some], some, o_win.at[b], e_win.at[b])

    for q in range(CHUNKS):
        arrive_long(1, q)
        arrive_short(1, q)
        if q == 1:
            choose_in_plane()
        if q == 2:
            scatter_z()

    count = SEGS * SEG_DEV
    up = (z == 0) & (core == 1)
    down = (z == RING - 1) & (core == 0)

    def edge(kv, device):
        return remote(
            near.at[S1 * BLK_DEV + 2 * core, kv], near.at[EDGE, kv], edge_s.at[kv], edge_r.at[kv], device
        )

    @pl.when(up)
    def _():
        for kv in range(2):
            edge(kv, (me + SEG_DEV - 1) % count).start()

    @pl.when(down)
    def _():
        for kv in range(2):
            edge(kv, (me + count - SEG_DEV + 1) % count).start()

    for q in range(CHUNKS):
        arrive_long(2, q)
        arrive_short(2, q)
        if q == 0:
            choose_in_ring()
        if q == 1:
            gather_z()
        if q == 4:
            spread_in_plane()
    for q in range(CHUNKS):
        for shard in (OWN, L1, S1, L2, S2):
            pair(shard, q).wait_recv()

    @pl.when((z == 0) & (core == 0) | (z == RING - 1) & (core == 1))
    def _():
        for kv in range(2):
            edge(kv, other).wait_recv()

    for copy, table in zip(tables, (tab_ss, tab_ls, tab_lo, tab_so)):
        copy.wait_recv()
    source = hop(2 * go_long) * 2 + core
    for twin, table in enumerate((tab_ss, tab_so)):
        block = S2 * BLK_DEV + wanted(table, source)
        for kv in range(2):
            stage3[twin, kv] = near[block, kv]
    load_q.wait()
    for kv in range(2):
        for twin in range(2):
            send_sel(0, twin, kv).start()

    @pl.loop(0, 3)
    def _(i):
        entry(i, 0)

    source = hop(3 * go_short) * 2 + core
    picks = [wanted(table, source) for table in (tab_ls, tab_lo)]
    for q in range(BLK_DEV):
        arrive_long(3, q)
    for twin in range(2):
        stage4[twin, 0] = l3k[picks[twin]]

    @pl.loop(1, PLANE)
    def _(i):
        to = (plane + i) % PLANE
        remote(cand.at[to], recv1.at[to], s1.at[to], r1.at[to], other).wait_send()
        remote(sel2, global_slot(slot), s4.at[to], r4.at[to], other).wait_send()

    for twin in range(2):
        send_sel(1, twin, 0).start()
    global_here()
    window(0)
    window(1)
    arrive_long(3, BLK_DEV)
    window(2)
    for q in range(BLK_DEV + 1, CHUNKS):
        arrive_long(3, q)
    for twin in range(2):
        stage4[twin, 1] = l3v[picks[twin]]
    for q in range(CHUNKS):
        long(1, q).wait_send()
        short(1, q).wait_send()
        pair(OWN, q).wait_send()
    for twin in range(2):
        send_sel(1, twin, 1).start()
    for q in range(CHUNKS):
        pair(L3, q).wait_recv()
    for kv in range(2):
        for twin in range(2):
            send_sel(0, twin, kv).wait_recv()

    @pl.loop(3, 7)
    def _(i):
        entry(i, 1)

    def merge(outs, logs):
        top = logs[0]
        for log in logs[1:]:
            top = jnp.maximum(top, log)
        weights = [jnp.exp2(log - top) for log in logs]
        total = sum(weights)
        return sum(weight * out for weight, out in zip(weights, outs)), total, top

    for b in range(BLK_DEV):
        rows = [ranks[b * RAND + r] for r in range(RAND)]
        for head_index in range(HEADS):
            cols = columns(head_index)
            outs = [o_win[b, :, cols]] + [jnp.where(r < 7, o_ent[r, :, cols], 0.0) for r in rows]
            logs = [e_win[b, :, cols]] + [jnp.where(r < 7, e_ent[r, :, cols], -jnp.inf) for r in rows]
            out, total, top = merge(outs, logs)
            o_win[b, :, cols] = out / total
            e_win[b, :, cols] = top + jnp.log2(total)

    for q in range(CHUNKS):
        for h in range(2, 4):
            long(h, q).wait_send()
        short(2, q).wait_send()
        for shard in range(1, 6):
            pair(shard, q).wait_send()
    for copy in tables:
        copy.wait_send()

    @pl.when(up | down)
    def _():
        for kv in range(2):
            edge(kv, other).wait_send()

    @pl.loop(0, RING)
    def _(to):
        there = sel1.at[:, cols_of(to)]
        remote(there, there, s2.at[to], r2.at[to], other).wait_send()
        remote(piece, piece, s3.at[to], r3.at[to], other).wait_send()

    load_w.wait()

    for twin in range(2):
        send_sel(1, twin, 0).wait_recv()
    ends = [entry_parts(i, 2) for i in range(7, ENTRIES)]
    halves = [first() for first, _ in ends]
    for twin in range(2):
        send_sel(1, twin, 1).wait_recv()
    for (_, second), half in zip(ends, halves):
        second(half)

    for b in range(BLK_DEV):
        here = [slots[i] % 4 == b for i in range(7, ENTRIES)]
        for head_index in range(HEADS):
            cols = columns(head_index)
            outs = [o_win[b, :, cols]] + [o_ent[i, :, cols] for i in range(7, ENTRIES)]
            logs = [e_win[b, :, cols]] + [
                jnp.where(at_b, e_ent[i, :, cols], -jnp.inf) for i, at_b in zip(range(7, ENTRIES), here)
            ]
            out, total, _ = merge(outs, logs)
            att[pl.ds(b * BLOCK, BLOCK), cols] = (out / total).astype(jnp.bfloat16)
    part = w_ref.shape[1] // 4
    for n in range(4):
        cols = pl.ds(n * part, part)
        out_ref[:, cols] = jnp.dot(att[...], w_ref[:, cols], preferred_element_type=jnp.float32).astype(jnp.bfloat16)
    for kv in range(2):
        for twin in range(2):
            send_sel(0, twin, kv).wait_send()
            send_sel(1, twin, kv).wait_send()


def put_kernel(x_ref, out_ref, sem):
    copy = pltpu.make_async_copy(x_ref, out_ref, sem)
    copy.start()
    copy.wait()


def put(x):
    return pl.pallas_call(
        put_kernel,
        out_shape=jax.ShapeDtypeStruct(x.shape, x.dtype),
        in_specs=[pl.BlockSpec(memory_space=pltpu.VMEM)],
        out_specs=pl.BlockSpec(memory_space=pltpu.HBM),
        scratch_shapes=[pltpu.SemaphoreType.DMA],
        compiler_params=pltpu.CompilerParams(vmem_limit_bytes=4 << 20),
        name="put",
    )(x)


def local(queries, keys_values, rand_blocks, global_ids, out_weight):
    width = queries.shape[1]
    depth = out_weight.shape[1]
    bf16, f32 = jnp.bfloat16, jnp.float32
    vmem, dma = pltpu.VMEM, pltpu.SemaphoreType.DMA
    table = pltpu.SMEM((BLK_DEV, RAND), jnp.int32)
    in_hbm = pl.BlockSpec(memory_space=pltpu.HBM)
    scalars = pl.BlockSpec(memory_space=pltpu.SMEM)
    out = pl.pallas_call(
        kernel,
        out_shape=pltpu.VMEM((BLK_DEV * BLOCK, depth), bf16),
        in_specs=[scalars, scalars, in_hbm, in_hbm, in_hbm],
        out_specs=pl.BlockSpec(memory_space=pltpu.VMEM),
        scratch_shapes=[
            vmem((EDGE + 1, 2, BLOCK, width), bf16),
            vmem((BLK_DEV, BLOCK, width), bf16),
            vmem((BLK_DEV, BLOCK, width), bf16),
            vmem((BLK_DEV + 2, 2, BLOCK, width), bf16),
            vmem((2, BLOCK, width), bf16),
            vmem((2, BLOCK, width), bf16),
            vmem((2, 2, BLOCK, width), bf16),
            vmem((2, 2, BLOCK, width), bf16),
            vmem((BLK_DEV, 2, BLOCK, width), bf16),
            vmem((PLANE, SLICE, width), bf16),
            vmem((PLANE, SLICE, width), bf16),
            vmem((RING, SLICE, 128), bf16),
            vmem((SLICE, width), bf16),
            vmem((SLICE, 128), bf16),
            vmem((SLICE, width), bf16),
            vmem((GLOB, 2, BLOCK, width), bf16),
            vmem((BLK_DEV, BLOCK, width), bf16),
            vmem((width, depth), bf16),
            vmem((ENTRIES, BLOCK, width), f32),
            vmem((ENTRIES, BLOCK, width), f32),
            vmem((BLK_DEV, BLOCK, width), f32),
            vmem((BLK_DEV, BLOCK, width), f32),
            vmem((BLK_DEV * BLOCK, width), bf16),
            table, table, table, table,
            pltpu.SMEM((ENTRIES,), jnp.int32),
            pltpu.SMEM((ENTRIES,), jnp.int32),
            dma((8,)),
            dma((3, CHUNKS)), dma((3, CHUNKS)),
            dma((2, CHUNKS)), dma((2, CHUNKS)),
            dma((2, 2, 2)), dma((2, 2, 2)),
            dma((6, CHUNKS)), dma((6, CHUNKS)),
            dma((4,)), dma((4,)),
            dma((2,)), dma((2,)),
            dma((PLANE,)), dma((PLANE,)),
            dma((RING,)), dma((RING,)),
            dma((RING,)), dma((RING,)),
            dma((PLANE,)), dma((PLANE,)),
            pltpu.SemaphoreType.REGULAR,
            pltpu.SemaphoreType.REGULAR,
            pltpu.SemaphoreType.REGULAR,
        ],
        compiler_params=pltpu.CompilerParams(
            collective_id=0, has_side_effects=True, vmem_limit_bytes=56 << 20
        ),
        name="sparse_attention",
    )(
        rand_blocks,
        global_ids,
        queries.reshape(BLK_DEV, BLOCK, width),
        keys_values.reshape(2, BLK_DEV, BLOCK, width),
        out_weight,
    )
    return put(out)


def solution(mesh):
    placed = (P("seq", None), P(None, "seq", None), P("seq", None), P(), P())
    return jax.shard_map(
        local, mesh=mesh, in_specs=placed, out_specs=P("seq", None), check_vma=False
    )
```
